32 devices in a mesh: dom: 16 (over z, y, x), ens: 2 (over core).
Axes of the slice: x: 2, y: 2, z: 4, core: 2. Of those that a mesh axis runs over, the one named last changes fastest.
Arguments:
- alpha: float32 [20, 4, 128, 512], P('ens', None, 'dom'), may hold values from -2.5 to 2.5
- perturb: bfloat16 [20, 4, 128, 512], P('ens', None, 'dom'), may hold values from -6 to 6
- static_ctl: float32 [4, 128, 512], P(None, 'dom'), may hold values from -6 to 6
- sigma: float32 [4, 128, 512], P(None, 'dom'), may hold values from 0.3 to 3
- class_index: int32 [4, 128, 512], P(None, 'dom'), may hold values from 0 to 7
- class_kappa: float32 [8], replicated, may hold values from 0.02 to 0.24
- obs_cell: int32 [32768], P('dom'), may hold values from 0 to 16383
- obs_value: float32 [32768], P('dom'), may hold values from -6 to 6
- obs_weight: float32 [32768], P('dom'), may hold values from 2 to 20
Outputs:
- grad_alpha: float32 [20, 4, 128, 512], P('ens', None, 'dom')
- grad_static: float32 [4, 128, 512], P(None, 'dom')
The draws below stay inside these ranges and needn't reach their ends.
Inputs may be any that keep to these rules, and one draw needn't show every extreme that they name: obs_cell[k] is a cell, in the order level, column, row, of the block of 8 columns that starts at column (k // 2048) * 8.
All inputs are finite; a program needn't handle non-finite values.
Results may differ from the reference program's by a relative error of at most 0.0005.
Values sent between devices are 32-bit elements; how exact they have to be, the bound alone decides.
A program may use at most 64 MiB of HBM per device.

```python
import math
import jax
import jax.numpy as jnp
from jax import lax

CX = 8
CY = 512
LEV = 4
NOBS_DEV = 2048
PASSES = 4
NCLASS = 8
MEMBERS = 20
NX = 128
NOBS = 32768


def plant(array, own_key, smallest, top_value):
    longest = array.shape.index(max(array.shape))
    spots = []
    for shift in (0, 1):
        where = [jax.random.randint(jax.random.fold_in(own_key, axis), (), 0, length) for axis, length in enumerate(array.shape)]
        where[longest] = (where[longest] + shift) % array.shape[longest]
        spots.append(tuple(where))
    return array.at[spots[0]].set(smallest).at[spots[1]].set(top_value)


def block_scale(stream_key, extent, pieces, smallest, high):
    factor_of, own = 1.0, jax.random.fold_in(stream_key, 6)
    for axis_at, shards_of in pieces:
        heights = jnp.exp(jax.random.uniform(jax.random.fold_in(own, axis_at), (shards_of,), jnp.float32, smallest / len(pieces), high / len(pieces)))
        factor_of = factor_of * jnp.repeat(heights, extent[axis_at] // shards_of).reshape([-1 if axis == axis_at else 1 for axis in range(len(extent))])
    return factor_of


def gaussian(key, extent, width, reach, split=(), held_as=jnp.bfloat16):
    result = jax.random.normal(key, extent, jnp.float32) * width
    if len(split) > 0:
        result = block_scale(key, extent, split, -0.22, 0.18) * result
    return jnp.clip(result, min=-reach, max=reach).astype(held_as)


def setup_inputs(seed: int = 0) -> dict:
    splits = jax.random.split(jax.random.key(seed), 10)
    return {
        "alpha": gaussian(splits[0], (MEMBERS, LEV, NX, CY), 0.3, 2.5, ((0, 2), (2, 16)), jnp.float32),
        "perturb": gaussian(splits[1], (MEMBERS, LEV, NX, CY), 1.0, 6.0, ((0, 2), (2, 16))),
        "static_ctl": gaussian(splits[2], (LEV, NX, CY), 1.0, 6.0, ((1, 16),), jnp.float32),
        "sigma": jnp.clip(jnp.exp(math.log(3.0) - 2.3025851 * jax.random.uniform(splits[3], (LEV, NX, CY), jnp.float32) ** block_scale(splits[3], (LEV, NX, CY), ((1, 16),), -0.2, 0.2)), 0.3, 3.0),
        "class_index": plant(jax.random.randint(splits[4], (LEV, NX, CY), 0, NCLASS), jax.random.fold_in(splits[4], 1), 0, NCLASS - 1).astype(jnp.int32),
        "class_kappa": jnp.clip(jax.random.uniform(splits[5], (NCLASS,), jnp.float32, 0.02, 0.24), 0.02, 0.24),
        "obs_cell": plant(jax.random.randint(splits[6], (NOBS,), 0, LEV * CX * CY), jax.random.fold_in(splits[6], 1), 0, (LEV * CX * CY) - 1).astype(jnp.int32),
        "obs_value": gaussian(splits[7], (NOBS,), 1.0, 6.0, ((0, 16),), jnp.float32),
        "obs_weight": jnp.clip(jnp.exp(math.log(20.0) - 2.3025851 * jax.random.uniform(splits[8], (NOBS,), jnp.float32) ** block_scale(splits[8], (NOBS,), ((0, 16),), -0.2, 0.2)), 2.0, 20.0),
    }


def one_pass(field, face_x, face_y):
    flux_x = face_x * (jnp.roll(field, -1, axis=-2) - field)
    flux_y = face_y * (field[..., 1:] - field[..., :-1])
    padded = jnp.pad(flux_y, [(0, 0)] * (flux_y.ndim - 1) + [(1, 1)])
    return field + (flux_x - jnp.roll(flux_x, 1, axis=-2)) + (padded[..., 1:] - padded[..., :-1])

def reference(alpha, perturb, static_ctl, sigma, class_index, class_kappa, obs_cell, obs_value, obs_weight):
    coeff = jnp.take(class_kappa, class_index)
    face_x = 0.5 * (coeff + jnp.roll(coeff, -1, axis=1))
    face_y = 0.5 * (coeff[..., :-1] + coeff[..., 1:])

    def diffuse(field):
        for index in range(PASSES):
            field = one_pass(field, face_x, face_y)
        return field
    scale = 1.0 / math.sqrt(MEMBERS - 1)

    def accumulate(total, member):
        return (total + member[1].astype(jnp.float32) * diffuse(member[0]), None)
    increment, unused = lax.scan(accumulate, jnp.zeros(static_ctl.shape, jnp.float32), (alpha, perturb))
    state = sigma * static_ctl + scale * increment
    plane = CX * CY
    block = (jnp.arange(obs_cell.shape[0], dtype=jnp.int32) // NOBS_DEV).astype(jnp.int32)
    level_index = obs_cell // plane
    remainder = obs_cell % plane
    column = block * CX + remainder // CY
    row_index = remainder % CY
    values = state[level_index, column, row_index]
    weighted = obs_weight * (values - obs_value)
    adjoint = jnp.zeros(static_ctl.shape, jnp.float32).at[level_index, column, row_index].add(weighted)
    grad_static = static_ctl + sigma * adjoint

    def member_grad(member):
        return member[0] + scale * diffuse(member[1].astype(jnp.float32) * adjoint)
    grad_alpha = lax.map(member_grad, (alpha, perturb))
    return (grad_alpha, grad_static)
```

```python
import functools
import math

import jax
import jax.numpy as jnp
from jax import lax
from jax.experimental import pallas as pl
from jax.experimental.pallas import tpu as pltpu
from jax.sharding import PartitionSpec as P

PASSES = 4
MESH = pl.DeviceIdType.MESH
LANES = 128
HALF = 256
PIECES = 3
CHUNKS = 4
f32 = jnp.float32
bf16 = jnp.bfloat16


def sub(shape):
    return lax.broadcasted_iota(jnp.int32, shape, len(shape) - 2)


def low_rows(shape):
    return sub(shape) < 4


def flip(x):
    return pltpu.roll(x, 4, 0)


def pair(a, b):
    return jnp.where(low_rows(a.shape), a, b)


def spread(x):
    other, low = flip(x), low_rows(x.shape)
    return jnp.where(low, x, other), jnp.where(low, other, x)


def sweep(start, fx, fy, first, last, emit):
    fields, fluxes = {}, {}

    def field(p, c):
        if (p, c) not in fields:
            fields[p, c] = start(c) if p == 0 else step(p - 1, c)
        return fields[p, c]

    def flux(p, c):
        if (p, c) not in fluxes:
            a, b = field(p, c), field(p, c + 1)
            if a is None and b is None:
                fluxes[p, c] = None
            elif a is None:
                fluxes[p, c] = fx[c] * b
            elif b is None:
                fluxes[p, c] = -(fx[c] * a)
            else:
                fluxes[p, c] = fx[c] * (b - a)
        return fluxes[p, c]

    def step(p, c):
        left, u, right = flux(p, c - 1), field(p, c), flux(p, c)
        if u is None:
            if left is None:
                return right
            return None if left is None and right is None else (-left if right is None else right - left)
        rows = u.shape[-1]
        up = fy[c] * (pltpu.roll(u, rows - 1, 1) - u)
        return u + (right - left) + (up - pltpu.roll(up, 1, 1))

    for c in range(first, last + 1):
        emit(c, field(PASSES, c))


def split3(x):
    out = []
    for _ in range(PIECES):
        out.append(x.astype(bf16).astype(f32))
        x = x - out[-1]
    return out


def block(v):
    return slice(v * LANES, (v + 1) * LANES)


def take(ref, at, count=8):
    return jnp.concatenate(
        [ref[v, pl.ds(at, count, stride=8), :] for v in range(ref.shape[0])], axis=1
    )


def put(ref, at, value):
    for v in range(ref.shape[0]):
        ref[v, pl.ds(at, value.shape[0], stride=8), :] = value[:, block(v)]


def lanes_of(t):
    return pl.ds(pl.multiple_of(t * LANES, LANES), LANES)


def hot_rows(cell, hot, t):
    low = (cell & (HALF - 1)).astype(f32)
    spot = lax.broadcasted_iota(jnp.int32, (HALF, LANES), 0).astype(f32)
    hot[:, lanes_of(t)] = jnp.where(spot == low, 1.0, 0.0).astype(bf16)


def exchange(
    n_dom, n_ens, scale,
    kappa_in, alpha_in, perturb_in, static_in, sigma_in, index_in, cell_in, value_in, weight_in,
    adj, ph, fx, fy, pf, alpha, static, sigma,
    kappa, index, perturb, cells, values, weights, twice, edge, known, p_send, p_recv, tail, total,
    shared, inc, beside, w_all, v_all, n_all, hot, x_all, wvn,
    in_sem, o_ss, o_rs, c_ss, c_rs, k_ss, k_rs, p_ss, p_rs, t_ss, t_rs, i_ss, i_rs,
):
    me, ens = lax.axis_index("dom"), lax.axis_index("ens")
    right, left = lax.rem(me + 1, n_dom), lax.rem(me + n_dom - 1, n_dom)
    rows = fx.shape[-1]
    groups = ph.shape[0]
    tiles = cells.shape[-1] // LANES
    per_chunk = tiles // CHUNKS
    sides = ((0, left), (1, right))

    loads = [
        pltpu.make_async_copy(src, dst, in_sem.at[i])
        for i, (src, dst) in enumerate((
            (index_in, index), (kappa_in, kappa), (cell_in, cells.at[2]), (perturb_in, perturb),
            (static_in, static), (sigma_in, sigma), (weight_in, weights.at[2]), (value_in, values.at[2]),
        ) + tuple((alpha_in.at[:, block(v)], alpha.at[v]) for v in range(alpha.shape[0])))
    ]
    for copy in loads:
        copy.start()

    barrier = pltpu.get_barrier_semaphore()
    for side in (left, right):
        pl.semaphore_signal(barrier, inc=1, device_id=(side, ens), device_id_type=MESH)
    for r in range(1, n_ens):
        pl.semaphore_signal(
            barrier, inc=1, device_id=(me, lax.rem(ens + r, n_ens)), device_id_type=MESH
        )
    pl.semaphore_wait(barrier, 2 + n_ens - 1)

    def send(src, dst, ss, rs, side):
        copy = pltpu.make_async_remote_copy(
            src_ref=src, dst_ref=dst, send_sem=ss, recv_sem=rs,
            device_id=(side, ens), device_id_type=MESH,
        )
        copy.start()
        return copy

    obs_copies = [
        send(src, dst.at[1 - s], o_ss.at[s, i], o_rs.at[1 - s, i], side)
        for i, (src, dst) in enumerate(
            ((cell_in, cells), (weight_in, weights), (value_in, values))
        )
        for s, side in sides
    ]

    def columns_of(field):
        for v in range(twice.shape[0]):
            twice[v, 0:32, :] = field[:, block(v)]
            twice[v, 32:64, :] = field[:, block(v)]
        return [take(twice, c) for c in range(8)]

    loads[0].wait()
    loads[1].wait()
    cls = index[...]
    coeff = jnp.zeros(cls.shape, f32)
    for number in range(kappa.shape[0]):
        coeff = jnp.where(cls == number, kappa[number], coeff)
    own = columns_of(coeff)
    for j in range(4):
        edge[2 + j] = pair(own[2 * j], own[2 * j + 1])
    edge_copies = [
        send(edge.at[pl.ds(2 + 2 * s, 2)], edge.at[pl.ds(6 - 6 * s, 2)], c_ss.at[s], c_rs.at[1 - s], side)
        for s, side in sides
    ]
    loads[2].wait()
    loads[3].wait()

    def collect(chunk, carry):
        for i in range(per_chunk):
            t = chunk * per_chunk + i
            hot_rows(cells[2, :, lanes_of(t)], hot.at[2], t)
        span = pl.ds(pl.multiple_of(chunk * per_chunk * LANES, LANES), per_chunk * LANES)
        found = [
            lax.dot_general(
                perturb[:, h * HALF : (h + 1) * HALF], hot[2, :, span],
                (((1,), (0,)), ((), ())), preferred_element_type=f32,
            )
            for h in range(2)
        ]
        column = sub((8, LANES)) * 2
        for i in range(per_chunk):
            key = lax.shift_right_logical(cells[2, :, lanes_of(chunk * per_chunk + i)], 8)
            masks = [[column + (16 * level + h) == key for h in range(2)] for level in range(4)]
            for m in range(2 * groups):
                kept = jnp.zeros((8, LANES), f32)
                for level in range(4):
                    for h in range(2):
                        at = (m * 4 + level) * 8
                        piece = found[h][at : at + 8, i * LANES : (i + 1) * LANES]
                        kept = jnp.where(masks[level][h], piece, kept)
                p_send[chunk, m // 2, m % 2 : m % 2 + 1, i * LANES : (i + 1) * LANES] = jnp.sum(
                    kept, axis=0, keepdims=True
                )
        for s, side in sides:
            send(p_send.at[chunk], p_recv.at[1 - s, chunk], p_ss.at[s, chunk], p_rs.at[1 - s, chunk], side)
        return carry

    lax.fori_loop(0, CHUNKS, collect, 0)

    loads[4].wait()
    loads[5].wait()
    own = columns_of(static[...] * sigma[...])
    for j in range(4):
        known[2 + j] = pair(own[2 * j], own[2 * j + 1])
    known_copies = [
        send(known.at[pl.ds(2 + 2 * s, 2)], known.at[pl.ds(6 - 6 * s, 2)], k_ss.at[s], k_rs.at[1 - s], side)
        for s, side in sides
    ]
    for v in range(pf.shape[0]):
        pf[v] = perturb[:, block(v)].astype(f32)

    for copy in edge_copies:
        copy.wait()
    inside = lax.broadcasted_iota(jnp.int32, (8, rows), 1) < rows - 1
    previous = None
    for j in range(8):
        for i, here in enumerate(spread(edge[j])):
            c = 2 * j + i
            fy[c] = jnp.where(inside, 0.5 * (here + pltpu.roll(here, rows - 1, 1)), 0.0)
            if previous is not None:
                fx[c - 1] = 0.5 * (previous + here)
            previous = here
    fx[15] = jnp.zeros((8, rows), f32)

    for copy in loads[8:]:
        copy.wait()
    total[...] = jnp.zeros(total.shape, f32)

    def forward(g, carry):
        def start(c):
            return take(alpha, g * 64 + c - 4) if 4 <= c < 12 else None

        def emit(c, out):
            if 4 <= c < 12:
                total[c - 4] += take(pf, g * 64 + c - 4) * out
            else:
                tail[g, c if c < 4 else c - 8] = out

        sweep(start, fx, fy, 0, 15, emit)
        return carry

    lax.fori_loop(0, groups, forward, 0)

    for copy in obs_copies:
        copy.wait()
    level_of = (sub((8, LANES)) % 4) * 16
    upper = sub((8, LANES)) < 4

    for chunk in range(CHUNKS):
        for s, side in sides:
            pltpu.make_async_remote_copy(
                src_ref=p_send.at[chunk], dst_ref=p_recv.at[1 - s, chunk],
                send_sem=p_ss.at[s, chunk], recv_sem=p_rs.at[1 - s, chunk],
                device_id=(side, ens), device_id_type=MESH,
            ).wait()

    for s in range(2):
        def place(t, carry):
            cell = cells[s, :, lanes_of(t)]
            hot_rows(cell, hot.at[s], t)
            key = lax.shift_right_logical(cell, 8)
            chunk, at = t // per_chunk, lanes_of(t % per_chunk)
            value = [
                jnp.where(upper, p_recv[s, chunk, g, 0:1, at], p_recv[s, chunk, g, 1:2, at])
                for g in range(groups)
            ]
            out = []
            for h in range(2):
                for c in range(4):
                    mask = level_of + (2 * (c + 4 - 4 * s) + h) == key
                    out += [jnp.where(mask, v, 0.0) for v in value]
            x_all[:, lanes_of(t)] = jnp.concatenate(out, axis=0).astype(bf16)
            return carry

        lax.fori_loop(0, tiles, place, 0)
        field = lax.dot_general(
            x_all[...], hot[s], (((1,), (1,)), ((), ())), preferred_element_type=f32
        )
        for h in range(2):
            for c in range(4):
                for g in range(groups):
                    at = ((h * 4 + c) * groups + g) * 8
                    ph[g, 4 * s + c, :, h * HALF : (h + 1) * HALF] = field[at : at + 8]

    def both(x):
        return x + flip(x)

    for j in range(4):
        sums = []
        for i in range(2):
            acc = jnp.zeros((8, rows), f32)
            for g in range(groups):
                acc = acc + ph[g, 2 * j + i] * tail[g, 2 * j + i]
            sums.append(both(acc))
        shared[0, j if j < 2 else j + 4] = pair(*sums)
        shared[0, 2 + j] = pair(both(total[2 * j]), both(total[2 * j + 1]))
    copies = []
    for r in range(1, n_ens):
        copy = pltpu.make_async_remote_copy(
            src_ref=shared.at[0], dst_ref=shared.at[r],
            send_sem=t_ss.at[r], recv_sem=t_rs.at[r],
            device_id=(me, lax.rem(ens + r, n_ens)), device_id_type=MESH,
        )
        copy.start()
        copies.append(copy)
    for copy in copies:
        copy.wait()
    whole = shared[lax.rem(ens + n_ens, n_ens)]
    for j in range(1, n_ens):
        whole = whole + shared[lax.rem(ens - j + n_ens, n_ens)]
    inc[...] = whole
    inc_copies = [
        send(inc.at[pl.ds(4 * s, 4)], beside.at[pl.ds(4 - 4 * s, 4)], i_ss.at[s], i_rs.at[1 - s], side)
        for s, side in sides
    ]

    loads[6].wait()
    loads[7].wait()
    order = (sub((8, LANES)) % 4) * 16 + (sub((8, LANES)) // 4) * 2
    for s in range(3):
        wide = 4 if s == 2 else 2
        first = 0 if s == 2 else 2 - 2 * s

        def weigh(t, carry):
            key = lax.shift_right_logical(cells[s, :, lanes_of(t)], 8)
            weight = weights[s, :, lanes_of(t)]
            pieces = split3(weight) + split3(weight * values[s, :, lanes_of(t)]) + [jnp.ones_like(weight)]
            masks = [order + (4 * (first + q) + h) == key for h in range(2) for q in range(wide)]
            out = [jnp.where(mask, piece, 0.0) for piece in pieces for mask in masks]
            wvn[0 : 8 * len(out), lanes_of(t)] = jnp.concatenate(out, axis=0).astype(bf16)
            return carry

        lax.fori_loop(0, tiles, weigh, 0)
        size = 16 * wide
        sums = lax.dot_general(
            wvn[0 : 7 * size, :], hot[s], (((1,), (1,)), ((), ())), preferred_element_type=f32
        )
        part = [sums[i * size : (i + 1) * size] for i in range(7)]
        at = (0, 6, 2)[s]
        for field, value in (
            (w_all, (part[2] + part[1]) + part[0]), (v_all, (part[5] + part[4]) + part[3]), (n_all, part[6])
        ):
            for h in range(2):
                for q in range(wide):
                    row = (h * wide + q) * 8
                    field[at + q, :, h * HALF : (h + 1) * HALF] = value[row : row + 8]

    for copy in known_copies + inc_copies:
        copy.wait()
    for j in range(8):
        once = 1.0 / jnp.maximum(n_all[j], 1.0)
        if 2 <= j < 6:
            state = known[j] + scale * (inc[j] + beside[j] * once)
            tile = w_all[j] * state - v_all[j]
        else:
            state = known[j] + scale * (inc[j] * once + beside[j])
            tile = (w_all[j] * state - v_all[j]) * once
        adj[2 * j], adj[2 * j + 1] = spread(tile)


def adjoint(scale, adj, ph, fx, fy, pf, alpha, static, sigma, ga, gs, out, natural, result, ga_sem, gs_sem):
    groups = ph.shape[0]
    for c in range(8):
        put(natural, c, adj[4 + c][0:4])
    result[...] = static[...] + sigma[...] * jnp.concatenate(
        [natural[v] for v in range(natural.shape[0])], axis=1
    )
    gs_copy = pltpu.make_async_copy(result, gs, gs_sem)
    gs_copy.start()

    def back(g, carry):
        def start(c):
            if 4 <= c < 12:
                return take(pf, g * 64 + c - 4) * adj[c]
            return ph[g, c if c < 4 else c - 8] * adj[c]

        def emit(c, u):
            at = g * 64 + c - 4
            put(out, at, take(alpha, at) + scale * u)

        sweep(start, fx, fy, 4, 11, emit)
        span = pl.ds(pl.multiple_of(g * 64, 64), 64)
        for v in range(out.shape[0]):
            pltpu.make_async_copy(out.at[v, span], ga.at[span, block(v)], ga_sem.at[g, v]).start()
        return carry

    lax.fori_loop(0, groups, back, 0)
    for g in range(groups):
        span = pl.ds(g * 64, 64)
        for v in range(out.shape[0]):
            pltpu.make_async_copy(out.at[v, span], ga.at[span, block(v)], ga_sem.at[g, v]).wait()
    gs_copy.wait()


def per_device(
    alpha, perturb, static_ctl, sigma, class_index, class_kappa, obs_cell, obs_value, obs_weight
):
    n_dom, n_ens = lax.axis_size("dom"), lax.axis_size("ens")
    local, levels, columns, rows = alpha.shape
    assert columns == 8 and levels == 4 and rows == 512 and local % 2 == 0
    scale = 1.0 / math.sqrt(local * n_ens - 1)
    count = obs_cell.shape[0]
    groups = local // 2
    flat = local * 32
    hbm = pl.BlockSpec(memory_space=pltpu.HBM)
    vmem = pl.BlockSpec(memory_space=pltpu.VMEM)
    dma = pltpu.SemaphoreType.DMA
    i32 = jnp.int32
    fields = (
        pltpu.VMEM((16, 8, rows), f32),
        pltpu.VMEM((groups, 8, 8, rows), f32),
        pltpu.VMEM((16, 8, rows), f32),
        pltpu.VMEM((16, 8, rows), f32),
        pltpu.VMEM((rows // LANES, flat, LANES), f32),
        pltpu.VMEM((rows // LANES, flat, LANES), f32),
        pltpu.VMEM((32, rows), f32),
        pltpu.VMEM((32, rows), f32),
    )
    passed = pl.pallas_call(
        functools.partial(exchange, n_dom, n_ens, scale),
        out_shape=fields,
        in_specs=[hbm] * 9,
        out_specs=(vmem,) * 8,
        scratch_shapes=[
            pltpu.SMEM(class_kappa.shape, f32),
            pltpu.VMEM((32, rows), i32),
            pltpu.VMEM((flat, rows), bf16),
            pltpu.VMEM((3, 1, count), i32),
            pltpu.VMEM((3, 1, count), f32),
            pltpu.VMEM((3, 1, count), f32),
            pltpu.VMEM((rows // LANES, 64, LANES), f32),
            pltpu.VMEM((8, 8, rows), f32),
            pltpu.VMEM((8, 8, rows), f32),
            pltpu.VMEM((CHUNKS, groups, 2, count // CHUNKS), f32),
            pltpu.VMEM((2, CHUNKS, groups, 2, count // CHUNKS), f32),
            pltpu.VMEM((groups, 8, 8, rows), f32),
            pltpu.VMEM((8, 8, rows), f32),
            pltpu.VMEM((n_ens, 8, 8, rows), f32),
            pltpu.VMEM((8, 8, rows), f32),
            pltpu.VMEM((8, 8, rows), f32),
            pltpu.VMEM((8, 8, rows), f32),
            pltpu.VMEM((8, 8, rows), f32),
            pltpu.VMEM((8, 8, rows), f32),
            pltpu.VMEM((3, HALF, count), bf16),
            pltpu.VMEM((flat, count), bf16),
            pltpu.VMEM((7 * 64, count), bf16),
            dma((8 + rows // LANES,)), dma((2, 3)), dma((2, 3)),
            dma((2,)), dma((2,)), dma((2,)), dma((2,)),
            dma((2, CHUNKS)), dma((2, CHUNKS)),
            dma((n_ens,)), dma((n_ens,)),
            dma((2,)), dma((2,)),
        ],
        compiler_params=pltpu.CompilerParams(
            collective_id=0, has_side_effects=True, vmem_limit_bytes=60 * 2**20
        ),
        name="exchange",
    )(
        class_kappa, alpha.reshape(flat, rows), perturb.reshape(flat, rows),
        static_ctl.reshape(32, rows), sigma.reshape(32, rows), class_index.reshape(32, rows),
        obs_cell.reshape(1, count), obs_value.reshape(1, count), obs_weight.reshape(1, count),
    )
    ga, gs = pl.pallas_call(
        functools.partial(adjoint, scale),
        out_shape=(
            jax.ShapeDtypeStruct((flat, rows), f32),
            jax.ShapeDtypeStruct((32, rows), f32),
        ),
        in_specs=[vmem] * 8,
        out_specs=(hbm,) * 2,
        scratch_shapes=[
            pltpu.VMEM((rows // LANES, flat, LANES), f32),
            pltpu.VMEM((rows // LANES, 32, LANES), f32),
            pltpu.VMEM((32, rows), f32),
            dma((groups, rows // LANES)), dma(()),
        ],
        compiler_params=pltpu.CompilerParams(vmem_limit_bytes=16 * 2**20),
        name="adjoint",
    )(*passed)
    return ga.reshape(alpha.shape), gs.reshape(static_ctl.shape)


def solution(mesh):
    return jax.shard_map(
        per_device,
        mesh=mesh,
        in_specs=(
            P("ens", None, "dom", None),
            P("ens", None, "dom", None),
            P(None, "dom", None),
            P(None, "dom", None),
            P(None, "dom", None),
            P(),
            P("dom"),
            P("dom"),
            P("dom"),
        ),
        out_specs=(P("ens", None, "dom", None), P(None, "dom", None)),
        check_vma=False,
    )
```

```python
import functools
import math

import jax
import jax.numpy as jnp
from jax import lax
from jax.experimental import pallas as pl
from jax.experimental.pallas import tpu as pltpu
from jax.sharding import PartitionSpec as P

PASSES = 4
MESH = pl.DeviceIdType.MESH
LANES = 128
HALF = 256
PIECES = 3
CHUNKS = 4
f32 = jnp.float32
bf16 = jnp.bfloat16


def sub(shape):
    return lax.broadcasted_iota(jnp.int32, shape, len(shape) - 2)


def low_rows(shape):
    return sub(shape) < 4


def flip(x):
    return pltpu.roll(x, 4, 0)


def pair(a, b):
    return jnp.where(low_rows(a.shape), a, b)


def spread(x):
    other, low = flip(x), low_rows(x.shape)
    return jnp.where(low, x, other), jnp.where(low, other, x)


def march(old, new, fx, fy, wrap, first, quads):
    groups = old.shape[1] // 8
    strips = fx.shape[-1] // LANES

    def get(ref, c, g=0):
        return [ref[c, 8 * g : 8 * g + 8, block(v)] for v in range(strips)]

    def body(i, left):
        c0 = first + 1 + 4 * i
        us = [[get(old, c0 + k, g) for g in range(groups)] for k in range(5)]
        after = [[pltpu.roll(us[k][g][0], LANES - 1, 1) for g in range(groups)] for k in range(4)]
        before = [[pltpu.roll(us[k][g][-1], 1, 1) for g in range(groups)] for k in range(4)]
        out = []
        for k in range(4):
            face, side, first_side = get(fx, c0 + k), get(fy, c0 + k), wrap[c0 + k]
            fluxes = []
            for g in range(groups):
                u, there = us[k][g], us[k + 1][g]
                right = [f * (b - a) for f, a, b in zip(face, u, there, strict=True)]
                up = [f * (b - a) for f, a, b in zip(side, u, u[1:] + [after[k][g]], strict=True)]
                down = [first_side * (u[0] - before[k][g])] + up[:-1]
                out.append([
                    a + (x - y) + (p - q)
                    for a, x, y, p, q in zip(u, right, left[g], up, down, strict=True)
                ])
                fluxes.append(right)
            left = fluxes
        for k in range(4):
            for g in range(groups):
                for v in range(strips):
                    new[c0 + k, 8 * g : 8 * g + 8, block(v)] = out[k * groups + g][v]
        return left

    start = [
        [f * (b - a) for f, a, b in zip(get(fx, first), get(old, first, g), get(old, first + 1, g), strict=True)]
        for g in range(groups)
    ]
    lax.fori_loop(0, quads, body, start)


def spot(cell):
    return (cell & -512) | ((cell & 3) << 7) | ((cell & 511) >> 2)


def order_rows(x, order):
    pieces = [piece.astype(bf16) for piece in split3(x)]
    return sum(jnp.dot(piece, order[...], preferred_element_type=f32) for piece in reversed(pieces))


def natural_rows(x, order):
    high = x.astype(bf16)
    low = (x - high.astype(f32)).astype(bf16)
    dims = (((1,), (1,)), ((), ()))
    return lax.dot_general(low, order[...], dims, preferred_element_type=f32) + lax.dot_general(
        high, order[...], dims, preferred_element_type=f32
    )


def split3(x):
    out = []
    for _ in range(PIECES):
        out.append(x.astype(bf16).astype(f32))
        x = x - out[-1]
    return out


def block(v):
    return slice(v * LANES, (v + 1) * LANES)


def take(ref, at, count=8):
    return jnp.concatenate(
        [ref[v, pl.ds(at, count, stride=8), :] for v in range(ref.shape[0])], axis=1
    )


def put(ref, at, value):
    for v in range(ref.shape[0]):
        ref[v, pl.ds(at, value.shape[0], stride=8), :] = value[:, block(v)]


def lanes_of(t):
    return pl.ds(pl.multiple_of(t * LANES, LANES), LANES)


def hot_rows(cell, hot, t):
    low = (cell & (HALF - 1)).astype(f32)
    spot = lax.broadcasted_iota(jnp.int32, (HALF, LANES), 0).astype(f32)
    hot[:, lanes_of(t)] = jnp.where(spot == low, 1.0, 0.0).astype(bf16)


def exchange(
    n_dom, n_ens, scale,
    kappa_in, alpha_in, perturb_in, static_in, sigma_in, index_in, cell_in, value_in, weight_in,
    adj, member, fx, fy, wrap, order, alpha, static, sigma,
    kappa, index, perturb, ordered, wide, natural, cells, values, weights, twice, edge, known, p_send, p_recv,
    field, shared, plain, tails, w_all, v_all, n_all, hot, x_all,
    in_sem, o_ss, o_rs, c_ss, c_rs, k_ss, k_rs, p_ss, p_rs, s_ss, s_rs, i_ss, i_rs, t_ss, t_rs, m_ss, m_rs,
):
    me, ens = lax.axis_index("dom"), lax.axis_index("ens")
    right, left = lax.rem(me + 1, n_dom), lax.rem(me + n_dom - 1, n_dom)
    rows = fx.shape[-1]
    strips = rows // LANES
    groups = member.shape[1] // 8
    deep = cells.shape[-1] // HALF
    sides = ((0, left), (1, right))

    barrier = pltpu.get_barrier_semaphore()
    for side in (left, right):
        for r in range(n_ens):
            pl.semaphore_signal(
                barrier, inc=1, device_id=(side, lax.rem(ens + r, n_ens)), device_id_type=MESH
            )
    for r in range(1, n_ens):
        pl.semaphore_signal(
            barrier, inc=1, device_id=(me, lax.rem(ens + r, n_ens)), device_id_type=MESH
        )

    loads = [
        pltpu.make_async_copy(src, dst, in_sem.at[i])
        for i, (src, dst) in enumerate((
            (index_in, index), (kappa_in, kappa), (cell_in, cells.at[2]), (perturb_in, perturb),
            (static_in, static), (sigma_in, sigma), (weight_in, weights.at[2]), (value_in, values.at[2]),
            (alpha_in, alpha),
        ))
    ]
    for copy in loads:
        copy.start()

    def send(src, dst, ss, rs, side, r=0):
        copy = pltpu.make_async_remote_copy(
            src_ref=src, dst_ref=dst, send_sem=ss, recv_sem=rs,
            device_id=(side, lax.rem(ens + r, n_ens)), device_id_type=MESH,
        )
        copy.start()
        return copy

    def swap(ref, ss, rs):
        return [
            send(ref.at[pl.ds(2 + 2 * s, 2)], ref.at[pl.ds(6 - 6 * s, 2)], ss.at[s], rs.at[1 - s], side)
            for s, side in sides
        ]

    def pairs_of(value, out):
        for v in range(strips):
            for level in range(4):
                tile = value(level, v)
                twice[v, 8 * level : 8 * level + 8, :] = tile
                twice[v, 32 + 8 * level : 40 + 8 * level, :] = tile
        for v in range(strips):
            for j in range(4):
                a, b = [twice[v, pl.ds(2 * j + i, 8, stride=8), :] for i in range(2)]
                out[2 + j, :, block(v)] = pair(a, b)

    zero = jnp.zeros((8, rows), f32)

    def sort_rows(v, carry):
        row = lax.broadcasted_iota(jnp.int32, (LANES, rows), 0) + v * LANES
        to = ((row & 3) << 7) | (row >> 2)
        here = lax.broadcasted_iota(jnp.int32, (LANES, rows), 1)
        order[pl.ds(pl.multiple_of(v * LANES, LANES), LANES), :] = jnp.where(to == here, 1.0, 0.0).astype(bf16)
        return carry

    lax.fori_loop(0, strips, sort_rows, 0)

    def clear(g, carry):
        at = pl.ds(pl.multiple_of(8 * g, 8), 8)
        for p, outer in ((0, (3, 4, 13, 14, 15, 16)), (1, (2, 3)), (2, (1, 2, 15, 16, 17, 18)), (3, (0, 1))):
            for c in outer:
                field[p, c, at] = zero
        return carry

    lax.fori_loop(0, groups, clear, 0)

    loads[0].wait()
    loads[1].wait()
    number = jnp.dot(index[...].astype(f32).astype(bf16), order[...], preferred_element_type=f32)

    def coefficient(level, v):
        mine = number[8 * level : 8 * level + 8, block(v)]
        out = jnp.zeros((8, LANES), f32)
        for k in range(kappa.shape[0]):
            out = jnp.where(mine == k, kappa[k], out)
        return out

    pairs_of(coefficient, edge)

    loads[3].wait()
    ordered[...] = jnp.dot(perturb[...], order[...], preferred_element_type=f32)
    perturb[...] = ordered[...].astype(bf16)
    loads[2].wait()

    def collect(n, carry):
        for i in range(4):
            hot_rows(spot(cells[2, :, lanes_of(4 * n + i)]), hot.at[2], 4 * n + i)
        span = pl.ds(pl.multiple_of(n * 2 * HALF, 2 * HALF), 2 * HALF)
        found = [
            lax.dot_general(
                perturb[:, h * HALF : (h + 1) * HALF], hot[2, :, span],
                (((1,), (0,)), ((), ())), preferred_element_type=f32,
            )
            for h in range(2)
        ]
        column = sub((8, LANES)) * 2
        for i in range(4):
            key = lax.shift_right_logical(spot(cells[2, :, lanes_of(4 * n + i)]), 8)
            masks = [[column + (16 * level + h) == key for h in range(2)] for level in range(4)]
            for m in range(2 * groups):
                kept = jnp.zeros((8, LANES), f32)
                for level in range(4):
                    for h in range(2):
                        at = (m * 4 + level) * 8
                        piece = found[h][at : at + 8, block(i)]
                        kept = jnp.where(masks[level][h], piece, kept)
                p_send[2 * n + i // 2, m // 2, m % 2 : m % 2 + 1, block(i % 2)] = jnp.sum(
                    kept, axis=0, keepdims=True
                )
        return carry

    lax.fori_loop(0, deep // 2, collect, 0)

    pl.semaphore_wait(barrier, 3 * n_ens - 1)
    edge_copies = swap(edge, c_ss, c_rs)

    def pass_on(src, dst, i):
        return [send(src, dst.at[1 - s], o_ss.at[s, i], o_rs.at[1 - s, i], side) for s, side in sides]

    cell_copies = pass_on(cell_in, cells, 0)
    p_copies = [
        send(p_send, p_recv.at[1 - s], p_ss.at[s], p_rs.at[1 - s], side) for s, side in sides
    ]
    weight_copies = pass_on(weight_in, weights, 1) + pass_on(value_in, values, 2)

    loads[4].wait()
    loads[5].wait()
    product = order_rows(static[...] * sigma[...], order)
    pairs_of(lambda level, v: product[8 * level : 8 * level + 8, block(v)], known)
    known_copies = swap(known, k_ss, k_rs)

    for v in range(strips):
        wide[v] = ordered[:, block(v)]

    def arrange(ref, at):
        def column(c, carry):
            for g in range(groups):
                ref[at + c, 8 * g : 8 * g + 8] = take(wide, g * 64 + c)
            return carry

        lax.fori_loop(0, 8, column, 0)

    arrange(member, 4)
    loads[8].wait()
    natural[...] = order_rows(alpha[...], order)
    for v in range(strips):
        wide[v] = natural[:, block(v)]
    arrange(field.at[0], 5)

    column_pairs = (sub((8, LANES)) % 4) * 16 + (sub((8, LANES)) // 4) * 2

    def weigh(q, carry):
        slot = jnp.where(q == 0, 0, jnp.where(q == 3, 1, 2))
        first = 2 * (1 - q % 2)

        def fill(t, carry):
            at = lanes_of(t)
            key = lax.shift_right_logical(spot(cells[slot, :, at]), 8)
            weight = weights[slot, :, at]
            pieces = split3(weight) + split3(weight * values[slot, :, at]) + [jnp.ones_like(weight)]
            masks = [column_pairs + (4 * (first + n) + h) == key for h in range(2) for n in range(2)]
            out = [jnp.where(mask, piece, 0.0) for piece in pieces for mask in masks]
            x_all[0 : 8 * len(out), at] = jnp.concatenate(out, axis=0).astype(bf16)
            return carry

        lax.fori_loop(0, 2 * deep, fill, 0)
        sums = lax.dot_general(
            x_all[0 : 7 * 32, :], hot[slot], (((1,), (1,)), ((), ())), preferred_element_type=f32
        )
        part = [sums[i * 32 : (i + 1) * 32] for i in range(7)]
        for ref, value in (
            (w_all, (part[2] + part[1]) + part[0]), (v_all, (part[5] + part[4]) + part[3]), (n_all, part[6])
        ):
            for h in range(2):
                for n in range(2):
                    row = (h * 2 + n) * 8
                    ref[2 * q + n, :, h * HALF : (h + 1) * HALF] = value[row : row + 8]
        return carry

    loads[6].wait()
    loads[7].wait()
    lax.fori_loop(1, 3, weigh, 0)

    for copy in edge_copies:
        copy.wait()
    lane = lax.broadcasted_iota(jnp.int32, (8, LANES), 1)

    def faces(j, previous):
        for i, here in enumerate(spread(edge[j])):
            c = 2 * j + i
            blocks = [here[:, block(v)] for v in range(strips)]
            after = blocks[1:] + [pltpu.roll(blocks[0], LANES - 1, 1)]
            up = [0.5 * (a + b) for a, b in zip(blocks, after, strict=True)]
            up[-1] = jnp.where(lane < LANES - 1, up[-1], 0.0)
            for v in range(strips):
                fy[c + 1, :, block(v)] = up[v]
            wrap[c + 1] = pltpu.roll(up[-1], 1, 1)
            fx[c] = 0.5 * (previous + here)
            previous = here
        return previous

    lax.fori_loop(0, 8, faces, zero)
    fx[0], fx[16], fx[17], fy[17], wrap[17] = zero, zero, zero, zero, zero[:, block(0)]

    def forward(p, carry):
        march(field.at[p], field.at[p + 1], fx, fy, wrap, 3 - p, (13 + 2 * p) // 4)
        return carry

    lax.fori_loop(0, PASSES, forward, 0)

    def both(x):
        return x + flip(x)

    def gather(j):
        sums = []
        for i in range(2):
            c = 2 * j + i
            acc = member[c, 0:8] * field[PASSES, c + 1, 0:8]
            for g in range(1, groups):
                acc = acc + member[c, 8 * g : 8 * g + 8] * field[PASSES, c + 1, 8 * g : 8 * g + 8]
            sums.append(both(acc))
        return pair(*sums)

    def inner(j, carry):
        shared[0, j] = gather(j + 2)
        return carry

    lax.fori_loop(0, 4, inner, 0)
    own_copies = [
        send(shared.at[0], shared.at[r], s_ss.at[r], s_rs.at[r], me, r) for r in range(1, n_ens)
    ]

    level_of = (sub((8, LANES)) % 4) * 16
    upper = sub((8, LANES)) < 4

    def tail_copies(s, side):
        return [
            pltpu.make_async_remote_copy(
                src_ref=tails.at[0, pl.ds(6 * s, 2)], dst_ref=tails.at[r, pl.ds(4 - 2 * s, 2)],
                send_sem=t_ss.at[s, r], recv_sem=t_rs.at[1 - s, r],
                device_id=(side, lax.rem(ens + r, n_ens)), device_id_type=MESH,
            )
            for r in range(n_ens)
        ] + [
            pltpu.make_async_remote_copy(
                src_ref=tails.at[0, pl.ds(6 * s, 2)], dst_ref=tails.at[r, pl.ds(6 * s, 2)],
                send_sem=m_ss.at[s, r], recv_sem=m_rs.at[s, r],
                device_id=(me, lax.rem(ens + r, n_ens)), device_id_type=MESH,
            )
            for r in range(1, n_ens)
        ]

    def beside(turn, carry):
        s = jnp.where(me == 0, 1 - turn, turn)
        away = jnp.where(s == 0, right, left)
        for src, dst, ss, rs in (
            (cell_in, cells.at[s], o_ss.at[1 - s, 0], o_rs.at[s, 0]),
            (p_send, p_recv.at[s], p_ss.at[1 - s], p_rs.at[s]),
        ):
            pltpu.make_async_remote_copy(
                src_ref=src, dst_ref=dst, send_sem=ss, recv_sem=rs,
                device_id=(away, ens), device_id_type=MESH,
            ).wait()

        def place(t, carry):
            cell = spot(cells[s, :, lanes_of(t)])
            hot_rows(cell, hot.at[s], t)
            key = lax.shift_right_logical(cell, 8)
            at = lanes_of(t % 2)
            value = [
                jnp.where(upper, p_recv[s, t // 2, g, 0:1, at], p_recv[s, t // 2, g, 1:2, at])
                for g in range(groups)
            ]
            out = []
            for h in range(2):
                for c in range(4):
                    mask = level_of + (2 * (c + 4 - 4 * s) + h) == key
                    out += [jnp.where(mask, v, 0.0) for v in value]
            x_all[:, lanes_of(t)] = jnp.concatenate(out, axis=0).astype(bf16)
            return carry

        lax.fori_loop(0, 2 * deep, place, 0)
        found = lax.dot_general(
            x_all[...], hot[s], (((1,), (1,)), ((), ())), preferred_element_type=f32
        )
        for h in range(2):
            for c in range(4):
                for g in range(groups):
                    at = ((h * 4 + c) * groups + g) * 8
                    member[12 * s + c, 8 * g : 8 * g + 8, h * HALF : (h + 1) * HALF] = found[at : at + 8]

        for j in range(2):
            tails[0, 6 * s + j] = gather(6 * s + j)
        for copy in tail_copies(s, jnp.where(s == 0, left, right)):
            copy.start()
        return carry

    lax.fori_loop(0, 2, beside, 0)

    for copy in own_copies:
        copy.wait()

    def settle(j, carry):
        whole = shared[lax.rem(ens + n_ens, n_ens), j]
        for e in range(1, n_ens):
            whole = whole + shared[lax.rem(ens - e + n_ens, n_ens), j]
        plain[2 + j] = whole
        return carry

    lax.fori_loop(0, 4, settle, 0)
    plain_copies = swap(plain, i_ss, i_rs)

    for copy in weight_copies:
        copy.wait()
    lax.fori_loop(0, 2, lambda i, carry: weigh(3 * i, carry), 0)

    for copy in known_copies + plain_copies + tail_copies(0, left) + tail_copies(1, right):
        copy.wait()

    def finish(j, carry):
        once = 1.0 / jnp.maximum(n_all[j], 1.0)
        whole = tails[lax.rem(ens + n_ens, n_ens), j]
        for e in range(1, n_ens):
            whole = whole + tails[lax.rem(ens - e + n_ens, n_ens), j]
        state = known[j] + scale * (plain[j] + whole * once)
        tile = w_all[j] * state - v_all[j]
        own = jnp.logical_and(j >= 2, j < 6)
        tile = jnp.where(own, tile, tile * once)
        adj[2 * j], adj[2 * j + 1] = spread(tile)
        return carry

    lax.fori_loop(0, 8, finish, 0)


def adjoint(
    scale, adj, member, fx, fy, wrap, order, alpha, static, sigma,
    ga, gs, out, wide, small, result, field, ga_sem, gs_sem,
):
    groups = member.shape[1] // 8
    strips = wide.shape[0]

    def begin(c, carry):
        one = adj[c]
        for g in range(groups):
            field[c + 1, 8 * g : 8 * g + 8] = member[c, 8 * g : 8 * g + 8] * one
        return carry

    lax.fori_loop(0, 16, begin, 0)

    def back(p, carry):
        march(field, field, fx, fy, wrap, p + 1, (17 - 2 * p) // 4)
        return carry

    lax.fori_loop(0, PASSES, back, 0)

    def end(c, carry):
        for g in range(groups):
            put(wide, g * 64 + c, field[5 + c, 8 * g : 8 * g + 8])
        put(small, c, adj[4 + c][0:4])
        return carry

    lax.fori_loop(0, 8, end, 0)

    def joined(ref, at):
        return jnp.concatenate([ref[v, at] for v in range(strips)], axis=1)

    part = 32 * groups
    copies = []
    for i in range(2):
        at = pl.ds(i * part, part)
        out[at] = alpha[at] + scale * natural_rows(joined(wide, at), order)
        copies.append(pltpu.make_async_copy(out.at[at], ga.at[at], ga_sem.at[i]))
        copies[-1].start()
    result[...] = static[...] + sigma[...] * natural_rows(joined(small, slice(None)), order)
    copies.append(pltpu.make_async_copy(result, gs, gs_sem))
    copies[-1].start()
    for copy in copies:
        copy.wait()


def per_device(
    alpha, perturb, static_ctl, sigma, class_index, class_kappa, obs_cell, obs_value, obs_weight
):
    n_dom, n_ens = lax.axis_size("dom"), lax.axis_size("ens")
    local, levels, columns, rows = alpha.shape
    assert columns == 8 and levels == 4 and rows == 512 and local % 2 == 0
    scale = 1.0 / math.sqrt(local * n_ens - 1)
    count = obs_cell.shape[0]
    groups = local // 2
    flat = local * 32
    tall = groups * 8
    strips = rows // LANES
    hbm = pl.BlockSpec(memory_space=pltpu.HBM)
    vmem = pl.BlockSpec(memory_space=pltpu.VMEM)
    dma = pltpu.SemaphoreType.DMA
    i32 = jnp.int32
    eight = pltpu.VMEM((8, 8, rows), f32)
    fields = (
        pltpu.VMEM((16, 8, rows), f32),
        pltpu.VMEM((16, tall, rows), f32),
        pltpu.VMEM((18, 8, rows), f32),
        pltpu.VMEM((18, 8, rows), f32),
        pltpu.VMEM((18, 8, LANES), f32),
        pltpu.VMEM((rows, rows), bf16),
        pltpu.VMEM((flat, rows), f32),
        pltpu.VMEM((32, rows), f32),
        pltpu.VMEM((32, rows), f32),
    )
    passed = pl.pallas_call(
        functools.partial(exchange, n_dom, n_ens, scale),
        out_shape=fields,
        in_specs=[hbm] * 9,
        out_specs=(vmem,) * len(fields),
        scratch_shapes=[
            pltpu.SMEM(class_kappa.shape, f32),
            pltpu.VMEM((32, rows), i32),
            pltpu.VMEM((flat, rows), bf16),
            pltpu.VMEM((flat, rows), f32),
            pltpu.VMEM((strips, flat, LANES), f32),
            pltpu.VMEM((flat, rows), f32),
            pltpu.VMEM((3, 1, count), i32),
            pltpu.VMEM((3, 1, count), f32),
            pltpu.VMEM((3, 1, count), f32),
            pltpu.VMEM((strips, 64, LANES), f32),
            eight,
            eight,
            pltpu.VMEM((count // HALF, groups, 2, HALF), f32),
            pltpu.VMEM((2, count // HALF, groups, 2, HALF), f32),
            pltpu.VMEM((PASSES + 1, 19, tall, rows), f32),
            pltpu.VMEM((n_ens, 4, 8, rows), f32),
            eight,
            pltpu.VMEM((n_ens, 8, 8, rows), f32),
            eight, eight, eight,
            pltpu.VMEM((3, HALF, count), bf16),
            pltpu.VMEM((flat, count), bf16),
            dma((9,)), dma((2, 3)), dma((2, 3)),
            dma((2,)), dma((2,)), dma((2,)), dma((2,)), dma((2,)), dma((2,)),
            dma((n_ens,)), dma((n_ens,)),
            dma((2,)), dma((2,)),
            dma((2, n_ens)), dma((2, n_ens)), dma((2, n_ens)), dma((2, n_ens)),
        ],
        compiler_params=pltpu.CompilerParams(
            collective_id=0, has_side_effects=True, vmem_limit_bytes=60 * 2**20
        ),
        name="exchange",
    )(
        class_kappa, alpha.reshape(flat, rows), perturb.reshape(flat, rows),
        static_ctl.reshape(32, rows), sigma.reshape(32, rows), class_index.reshape(32, rows),
        obs_cell.reshape(1, count), obs_value.reshape(1, count), obs_weight.reshape(1, count),
    )
    ga, gs = pl.pallas_call(
        functools.partial(adjoint, scale),
        out_shape=(
            jax.ShapeDtypeStruct((flat, rows), f32),
            jax.ShapeDtypeStruct((32, rows), f32),
        ),
        in_specs=[vmem] * len(fields),
        out_specs=(hbm,) * 2,
        scratch_shapes=[
            pltpu.VMEM((flat, rows), f32),
            pltpu.VMEM((strips, flat, LANES), f32),
            pltpu.VMEM((strips, 32, LANES), f32),
            pltpu.VMEM((32, rows), f32),
            pltpu.VMEM((19, tall, rows), f32),
            dma((2,)), dma(()),
        ],
        compiler_params=pltpu.CompilerParams(vmem_limit_bytes=24 * 2**20),
        name="adjoint",
    )(*passed)
    return ga.reshape(alpha.shape), gs.reshape(static_ctl.shape)


def solution(mesh):
    return jax.shard_map(
        per_device,
        mesh=mesh,
        in_specs=(
            P("ens", None, "dom", None),
            P("ens", None, "dom", None),
            P(None, "dom", None),
            P(None, "dom", None),
            P(None, "dom", None),
            P(),
            P("dom"),
            P("dom"),
            P("dom"),
        ),
        out_specs=(P("ens", None, "dom", None), P(None, "dom", None)),
        check_vma=False,
    )
```

```python
import functools
import math

import jax
import jax.numpy as jnp
from jax import lax
from jax.experimental import pallas as pl
from jax.experimental.pallas import tpu as pltpu
from jax.sharding import PartitionSpec as P

PASSES = 4
MESH = pl.DeviceIdType.MESH
LANES = 128
HALF = 256
PIECES = 3
CHUNKS = 4
f32 = jnp.float32
bf16 = jnp.bfloat16


def sub(shape):
    return lax.broadcasted_iota(jnp.int32, shape, len(shape) - 2)


def low_rows(shape):
    return sub(shape) < 4


def flip(x):
    return pltpu.roll(x, 4, 0)


def pair(a, b):
    return jnp.where(low_rows(a.shape), a, b)


def spread(x):
    other, low = flip(x), low_rows(x.shape)
    return jnp.where(low, x, other), jnp.where(low, other, x)


def march(old, new, fx, fy, wrap, first, quads):
    groups = old.shape[1] // 8
    strips = fx.shape[-1] // LANES

    def get(ref, c, g=0):
        return [ref[c, 8 * g : 8 * g + 8, block(v)] for v in range(strips)]

    def body(i, left):
        c0 = first + 1 + 4 * i
        us = [[get(old, c0 + k, g) for g in range(groups)] for k in range(5)]
        after = [[pltpu.roll(us[k][g][0], LANES - 1, 1) for g in range(groups)] for k in range(4)]
        before = [[pltpu.roll(us[k][g][-1], 1, 1) for g in range(groups)] for k in range(4)]
        out = []
        for k in range(4):
            face, side, first_side = get(fx, c0 + k), get(fy, c0 + k), wrap[c0 + k]
            fluxes = []
            for g in range(groups):
                u, there = us[k][g], us[k + 1][g]
                right = [f * (b - a) for f, a, b in zip(face, u, there, strict=True)]
                up = [f * (b - a) for f, a, b in zip(side, u, u[1:] + [after[k][g]], strict=True)]
                down = [first_side * (u[0] - before[k][g])] + up[:-1]
                out.append([
                    a + (x - y) + (p - q)
                    for a, x, y, p, q in zip(u, right, left[g], up, down, strict=True)
                ])
                fluxes.append(right)
            left = fluxes
        for k in range(4):
            for g in range(groups):
                for v in range(strips):
                    new[c0 + k, 8 * g : 8 * g + 8, block(v)] = out[k * groups + g][v]
        return left

    start = [
        [f * (b - a) for f, a, b in zip(get(fx, first), get(old, first, g), get(old, first + 1, g), strict=True)]
        for g in range(groups)
    ]
    lax.fori_loop(0, quads, body, start)


def spot(cell):
    return (cell & -512) | ((cell & 3) << 7) | ((cell & 511) >> 2)


def order_rows(x, order):
    pieces = [piece.astype(bf16) for piece in split3(x)]
    return sum(jnp.dot(piece, order[...], preferred_element_type=f32) for piece in reversed(pieces))


def natural_rows(x, order):
    high = x.astype(bf16)
    low = (x - high.astype(f32)).astype(bf16)
    dims = (((1,), (1,)), ((), ()))
    return lax.dot_general(low, order[...], dims, preferred_element_type=f32) + lax.dot_general(
        high, order[...], dims, preferred_element_type=f32
    )


def split3(x):
    out = []
    for _ in range(PIECES):
        out.append(x.astype(bf16).astype(f32))
        x = x - out[-1]
    return out


def block(v):
    return slice(v * LANES, (v + 1) * LANES)


def take(ref, at, count=8):
    return jnp.concatenate(
        [ref[v, pl.ds(at, count, stride=8), :] for v in range(ref.shape[0])], axis=1
    )


def put(ref, at, value):
    for v in range(ref.shape[0]):
        ref[v, pl.ds(at, value.shape[0], stride=8), :] = value[:, block(v)]


def lanes_of(t):
    return pl.ds(pl.multiple_of(t * LANES, LANES), LANES)


def hot_rows(cell, hot, t):
    low = (cell & (HALF - 1)).astype(f32)
    spot = lax.broadcasted_iota(jnp.int32, (HALF, LANES), 0).astype(f32)
    hot[:, lanes_of(t)] = jnp.where(spot == low, 1.0, 0.0).astype(bf16)


def exchange(
    n_dom, n_ens, scale,
    kappa_in, alpha_in, perturb_in, static_in, sigma_in, index_in, cell_in, value_in, weight_in,
    adj, member, fx, fy, wrap, order, alpha, static, sigma,
    kappa, index, perturb, ordered, wide, natural, cells, values, weights, twice, edge, known, p_send, p_recv,
    field, shared, plain, tails, w_all, v_all, n_all, hot, x_all,
    in_sem, o_ss, o_rs, c_ss, c_rs, k_ss, k_rs, p_ss, p_rs, s_ss, s_rs, i_ss, i_rs, t_ss, t_rs, m_ss, m_rs,
):
    me, ens = lax.axis_index("dom"), lax.axis_index("ens")
    right, left = lax.rem(me + 1, n_dom), lax.rem(me + n_dom - 1, n_dom)
    rows = fx.shape[-1]
    strips = rows // LANES
    groups = member.shape[1] // 8
    deep = cells.shape[-1] // HALF
    sides = ((0, left), (1, right))

    barrier = pltpu.get_barrier_semaphore()
    for side in (left, right):
        for r in range(n_ens):
            pl.semaphore_signal(
                barrier, inc=1, device_id=(side, lax.rem(ens + r, n_ens)), device_id_type=MESH
            )
    for r in range(1, n_ens):
        pl.semaphore_signal(
            barrier, inc=1, device_id=(me, lax.rem(ens + r, n_ens)), device_id_type=MESH
        )

    loads = [
        pltpu.make_async_copy(src, dst, in_sem.at[i])
        for i, (src, dst) in enumerate((
            (index_in, index), (kappa_in, kappa), (cell_in, cells.at[2]), (perturb_in, perturb),
            (static_in, static), (sigma_in, sigma), (weight_in, weights.at[2]), (value_in, values.at[2]),
            (alpha_in, alpha),
        ))
    ]
    for copy in loads:
        copy.start()

    def remote(src, dst, ss, rs, side, r=0):
        return pltpu.make_async_remote_copy(
            src_ref=src, dst_ref=dst, send_sem=ss, recv_sem=rs,
            device_id=(side, lax.rem(ens + r, n_ens)), device_id_type=MESH,
        )

    def started(copies):
        for copy in copies:
            copy.start()
        return copies

    def swap(ref, ss, rs):
        return [
            remote(ref.at[pl.ds(2 + 2 * s, 2)], ref.at[pl.ds(6 - 6 * s, 2)], ss.at[s], rs.at[1 - s], side)
            for s, side in sides
        ]

    def pairs_of(value, out):
        for v in range(strips):
            for level in range(4):
                tile = value(level, v)
                twice[v, 8 * level : 8 * level + 8, :] = tile
                twice[v, 32 + 8 * level : 40 + 8 * level, :] = tile
        for v in range(strips):
            for j in range(4):
                a, b = [twice[v, pl.ds(2 * j + i, 8, stride=8), :] for i in range(2)]
                out[2 + j, :, block(v)] = pair(a, b)

    zero = jnp.zeros((8, rows), f32)

    def sort_rows(v, carry):
        row = lax.broadcasted_iota(jnp.int32, (LANES, rows), 0) + v * LANES
        to = ((row & 3) << 7) | (row >> 2)
        here = lax.broadcasted_iota(jnp.int32, (LANES, rows), 1)
        order[pl.ds(pl.multiple_of(v * LANES, LANES), LANES), :] = jnp.where(to == here, 1.0, 0.0).astype(bf16)
        return carry

    lax.fori_loop(0, strips, sort_rows, 0)

    def clear(g, carry):
        at = pl.ds(pl.multiple_of(8 * g, 8), 8)
        for p, outer in ((0, (3, 4, 13, 14, 15, 16)), (1, (2, 3)), (2, (1, 2, 15, 16, 17, 18)), (3, (0, 1))):
            for c in outer:
                field[p, c, at] = zero
        return carry

    lax.fori_loop(0, groups, clear, 0)

    loads[0].wait()
    loads[1].wait()
    number = jnp.dot(index[...].astype(f32).astype(bf16), order[...], preferred_element_type=f32)

    def coefficient(level, v):
        mine = number[8 * level : 8 * level + 8, block(v)]
        out = jnp.zeros((8, LANES), f32)
        for k in range(kappa.shape[0]):
            out = jnp.where(mine == k, kappa[k], out)
        return out

    pairs_of(coefficient, edge)

    def pass_on(src, dst, i):
        return [remote(src, dst.at[1 - s], o_ss.at[s, i], o_rs.at[1 - s, i], side) for s, side in sides]

    edge_copies = swap(edge, c_ss, c_rs)
    first_copies = edge_copies + pass_on(cell_in, cells, 0)

    def greet(now):
        @pl.when(now)
        def _():
            pl.semaphore_wait(barrier, 3 * n_ens - 1)
            for copy in first_copies:
                copy.start()

    greet(me != 0)
    loads[3].wait()
    ordered[...] = jnp.dot(perturb[...], order[...], preferred_element_type=f32)
    perturb[...] = ordered[...].astype(bf16)
    loads[2].wait()

    def collect(n, carry):
        for i in range(4):
            hot_rows(spot(cells[2, :, lanes_of(4 * n + i)]), hot.at[2], 4 * n + i)
        span = pl.ds(pl.multiple_of(n * 2 * HALF, 2 * HALF), 2 * HALF)
        found = [
            lax.dot_general(
                perturb[:, h * HALF : (h + 1) * HALF], hot[2, :, span],
                (((1,), (0,)), ((), ())), preferred_element_type=f32,
            )
            for h in range(2)
        ]
        column = sub((8, LANES)) * 2
        for i in range(4):
            key = lax.shift_right_logical(spot(cells[2, :, lanes_of(4 * n + i)]), 8)
            masks = [[column + (16 * level + h) == key for h in range(2)] for level in range(4)]
            for m in range(2 * groups):
                kept = jnp.zeros((8, LANES), f32)
                for level in range(4):
                    for h in range(2):
                        at = (m * 4 + level) * 8
                        piece = found[h][at : at + 8, block(i)]
                        kept = jnp.where(masks[level][h], piece, kept)
                p_send[2 * n + i // 2, m // 2, m % 2 : m % 2 + 1, block(i % 2)] = jnp.sum(
                    kept, axis=0, keepdims=True
                )
        return carry

    def p_copy(s, side, n):
        part = pl.ds(2 * n, 2)
        return remote(p_send.at[part], p_recv.at[1 - s, part], p_ss.at[s, n], p_rs.at[1 - s, n], side)

    def collect_and_send(n, carry):
        collect(n, carry)

        @pl.when(me != 0)
        def _():
            started([p_copy(s, side, n) for s, side in sides])

        return carry

    lax.fori_loop(0, deep // 2, collect_and_send, 0)

    greet(me == 0)
    pl.when(me == 0)(lambda: started([p_copy(0, left, n) for n in range(deep // 2)]) and None)

    loads[4].wait()
    loads[5].wait()
    product = order_rows(static[...] * sigma[...], order)
    pairs_of(lambda level, v: product[8 * level : 8 * level + 8, block(v)], known)
    pl.when(me == 0)(lambda: started([p_copy(1, right, n) for n in range(deep // 2)]) and None)

    for v in range(strips):
        wide[v] = ordered[:, block(v)]

    def arrange(ref, at):
        def column(c, carry):
            for g in range(groups):
                ref[at + c, 8 * g : 8 * g + 8] = take(wide, g * 64 + c)
            return carry

        lax.fori_loop(0, 8, column, 0)

    arrange(member, 4)
    loads[8].wait()
    natural[...] = order_rows(alpha[...], order)
    for v in range(strips):
        wide[v] = natural[:, block(v)]
    arrange(field.at[0], 5)

    column_pairs = (sub((8, LANES)) % 4) * 16 + (sub((8, LANES)) // 4) * 2

    def weigh(q, carry):
        slot = jnp.where(q == 0, 0, jnp.where(q == 3, 1, 2))
        first = 2 * (1 - q % 2)

        def fill(t, carry):
            at = lanes_of(t)
            key = lax.shift_right_logical(spot(cells[slot, :, at]), 8)
            weight = weights[slot, :, at]
            pieces = split3(weight) + split3(weight * values[slot, :, at]) + [jnp.ones_like(weight)]
            masks = [column_pairs + (4 * (first + n) + h) == key for h in range(2) for n in range(2)]
            out = [jnp.where(mask, piece, 0.0) for piece in pieces for mask in masks]
            x_all[0 : 8 * len(out), at] = jnp.concatenate(out, axis=0).astype(bf16)
            return carry

        lax.fori_loop(0, 2 * deep, fill, 0)
        sums = lax.dot_general(
            x_all[0 : 7 * 32, :], hot[slot], (((1,), (1,)), ((), ())), preferred_element_type=f32
        )
        part = [sums[i * 32 : (i + 1) * 32] for i in range(7)]
        for ref, value in (
            (w_all, (part[2] + part[1]) + part[0]), (v_all, (part[5] + part[4]) + part[3]), (n_all, part[6])
        ):
            for h in range(2):
                for n in range(2):
                    row = (h * 2 + n) * 8
                    ref[2 * q + n, :, h * HALF : (h + 1) * HALF] = value[row : row + 8]
        return carry

    loads[6].wait()
    loads[7].wait()
    lax.fori_loop(1, 3, weigh, 0)

    lane = lax.broadcasted_iota(jnp.int32, (8, LANES), 1)

    def faces(j, previous):
        for i, here in enumerate(spread(edge[j])):
            c = 2 * j + i
            blocks = [here[:, block(v)] for v in range(strips)]
            after = blocks[1:] + [pltpu.roll(blocks[0], LANES - 1, 1)]
            up = [0.5 * (a + b) for a, b in zip(blocks, after, strict=True)]
            up[-1] = jnp.where(lane < LANES - 1, up[-1], 0.0)
            for v in range(strips):
                fy[c + 1, :, block(v)] = up[v]
            wrap[c + 1] = pltpu.roll(up[-1], 1, 1)
            fx[c] = 0.5 * (previous + here)
            previous = here
        return previous


    def forward(p, carry):
        march(field.at[p], field.at[p + 1], fx, fy, wrap, 3 - p, (13 + 2 * p) // 4)
        return carry

    def both(x):
        return x + flip(x)

    def gather(j):
        sums = []
        for i in range(2):
            c = 2 * j + i
            acc = member[c, 0:8] * field[PASSES, c + 1, 0:8]
            for g in range(1, groups):
                acc = acc + member[c, 8 * g : 8 * g + 8] * field[PASSES, c + 1, 8 * g : 8 * g + 8]
            sums.append(both(acc))
        return pair(*sums)

    def inner(j, carry):
        shared[0, j] = gather(j + 2)
        return carry

    own_copies = [
        remote(shared.at[0], shared.at[r], s_ss.at[r], s_rs.at[r], me, r) for r in range(1, n_ens)
    ]

    def spread_alpha():
        for copy in edge_copies:
            copy.wait()
        lax.fori_loop(0, 8, faces, zero)
        fx[0], fx[16], fx[17], fy[17], wrap[17] = zero, zero, zero, zero, zero[:, block(0)]
        lax.fori_loop(0, PASSES, forward, 0)
        lax.fori_loop(0, 4, inner, 0)
        started(own_copies)

    level_of = (sub((8, LANES)) % 4) * 16
    upper = sub((8, LANES)) < 4

    def tail_copies(s, side):
        return [
            pltpu.make_async_remote_copy(
                src_ref=tails.at[0, pl.ds(6 * s, 2)], dst_ref=tails.at[r, pl.ds(4 - 2 * s, 2)],
                send_sem=t_ss.at[s, r], recv_sem=t_rs.at[1 - s, r],
                device_id=(side, lax.rem(ens + r, n_ens)), device_id_type=MESH,
            )
            for r in range(n_ens)
        ] + [
            pltpu.make_async_remote_copy(
                src_ref=tails.at[0, pl.ds(6 * s, 2)], dst_ref=tails.at[r, pl.ds(6 * s, 2)],
                send_sem=m_ss.at[s, r], recv_sem=m_rs.at[s, r],
                device_id=(me, lax.rem(ens + r, n_ens)), device_id_type=MESH,
            )
            for r in range(1, n_ens)
        ]

    plain_copies = swap(plain, i_ss, i_rs)

    def settle():
        for copy in own_copies:
            copy.wait()
        for j in range(4):
            whole = shared[lax.rem(ens + n_ens, n_ens), j]
            for e in range(1, n_ens):
                whole = whole + shared[lax.rem(ens - e + n_ens, n_ens), j]
            plain[2 + j] = whole
        started(plain_copies)

    final = me == n_dom - 1

    def beside(s, i):
        away = jnp.where(s == 0, right, left)
        remote(cell_in, cells.at[s], o_ss.at[1 - s, 0], o_rs.at[s, 0], away).wait()

        def place(t, carry):
            cell = spot(cells[s, :, lanes_of(t)])
            hot_rows(cell, hot.at[s], t)
            key = lax.shift_right_logical(cell, 8)
            at = lanes_of(t % 2)
            value = [
                jnp.where(upper, p_recv[s, t // 2, g, 0:1, at], p_recv[s, t // 2, g, 1:2, at])
                for g in range(groups)
            ]
            out = []
            for h in range(2):
                for c in range(4):
                    mask = level_of + (2 * (c + 4 - 4 * s) + h) == key
                    out += [jnp.where(mask, v, 0.0) for v in value]
            x_all[:, lanes_of(t)] = jnp.concatenate(out, axis=0).astype(bf16)
            return carry

        def part(n, carry):
            p_copy(1 - s, away, n).wait()
            return lax.fori_loop(4 * n, 4 * n + 4, place, carry)

        lax.fori_loop(0, deep // 2, part, 0)
        pl.when(i == jnp.where(final, 2, 1))(settle)
        found = lax.dot_general(
            x_all[...], hot[s], (((1,), (1,)), ((), ())), preferred_element_type=f32
        )
        for h in range(2):
            for c in range(4):
                for g in range(groups):
                    at = ((h * 4 + c) * groups + g) * 8
                    member[12 * s + c, 8 * g : 8 * g + 8, h * HALF : (h + 1) * HALF] = found[at : at + 8]


    def phase(i, carry):
        stencil = i == jnp.where(final, 1, 0)
        s = jnp.where(final, i // 2, jnp.where(me < 2, 2 - i, i - 1))
        pl.when(stencil)(spread_alpha)
        pl.when(jnp.logical_not(stencil))(lambda: beside(s, i))

        def tail(n, carry):
            out = jnp.where(final, 1 - n, s)
            for j in range(2):
                tails[0, 6 * out + j] = gather(6 * out + j)
            started(tail_copies(out, jnp.where(out == 0, left, right)))
            return carry

        lax.fori_loop(0, jnp.where(final, i // 2 * 2, jnp.minimum(i, 1)), tail, 0)
        return carry

    weight_copies = started(pass_on(weight_in, weights, 1) + pass_on(value_in, values, 2))
    known_copies = started(swap(known, k_ss, k_rs))
    lax.fori_loop(0, 3, phase, 0)

    for copy in weight_copies:
        copy.wait()
    lax.fori_loop(0, 2, lambda i, carry: weigh(3 * i, carry), 0)

    for copy in known_copies + plain_copies + tail_copies(0, left) + tail_copies(1, right):
        copy.wait()

    def finish(j, carry):
        once = 1.0 / jnp.maximum(n_all[j], 1.0)
        whole = tails[lax.rem(ens + n_ens, n_ens), j]
        for e in range(1, n_ens):
            whole = whole + tails[lax.rem(ens - e + n_ens, n_ens), j]
        state = known[j] + scale * (plain[j] + whole * once)
        tile = w_all[j] * state - v_all[j]
        own = jnp.logical_and(j >= 2, j < 6)
        tile = jnp.where(own, tile, tile * once)
        adj[2 * j], adj[2 * j + 1] = spread(tile)
        return carry

    lax.fori_loop(0, 8, finish, 0)


def adjoint(
    scale, adj, member, fx, fy, wrap, order, alpha, static, sigma,
    ga, gs, out, wide, small, result, field, ga_sem, gs_sem,
):
    groups = member.shape[1] // 8
    strips = wide.shape[0]

    def begin(c, carry):
        one = adj[c]
        for g in range(groups):
            field[c + 1, 8 * g : 8 * g + 8] = member[c, 8 * g : 8 * g + 8] * one
        return carry

    lax.fori_loop(0, 16, begin, 0)

    def back(p, carry):
        march(field, field, fx, fy, wrap, p + 1, (17 - 2 * p) // 4)
        return carry

    lax.fori_loop(0, PASSES, back, 0)

    def end(c, carry):
        for g in range(groups):
            put(wide, g * 64 + c, field[5 + c, 8 * g : 8 * g + 8])
        put(small, c, adj[4 + c][0:4])
        return carry

    lax.fori_loop(0, 8, end, 0)

    def joined(ref, at):
        return jnp.concatenate([ref[v, at] for v in range(strips)], axis=1)

    part = 32 * groups
    copies = []
    for i in range(2):
        at = pl.ds(i * part, part)
        out[at] = alpha[at] + scale * natural_rows(joined(wide, at), order)
        copies.append(pltpu.make_async_copy(out.at[at], ga.at[at], ga_sem.at[i]))
        copies[-1].start()
    result[...] = static[...] + sigma[...] * natural_rows(joined(small, slice(None)), order)
    copies.append(pltpu.make_async_copy(result, gs, gs_sem))
    copies[-1].start()
    for copy in copies:
        copy.wait()


def per_device(
    alpha, perturb, static_ctl, sigma, class_index, class_kappa, obs_cell, obs_value, obs_weight
):
    n_dom, n_ens = lax.axis_size("dom"), lax.axis_size("ens")
    local, levels, columns, rows = alpha.shape
    assert columns == 8 and levels == 4 and rows == 512 and local % 2 == 0
    scale = 1.0 / math.sqrt(local * n_ens - 1)
    count = obs_cell.shape[0]
    groups = local // 2
    flat = local * 32
    tall = groups * 8
    strips = rows // LANES
    hbm = pl.BlockSpec(memory_space=pltpu.HBM)
    vmem = pl.BlockSpec(memory_space=pltpu.VMEM)
    dma = pltpu.SemaphoreType.DMA
    i32 = jnp.int32
    eight = pltpu.VMEM((8, 8, rows), f32)
    fields = (
        pltpu.VMEM((16, 8, rows), f32),
        pltpu.VMEM((16, tall, rows), f32),
        pltpu.VMEM((18, 8, rows), f32),
        pltpu.VMEM((18, 8, rows), f32),
        pltpu.VMEM((18, 8, LANES), f32),
        pltpu.VMEM((rows, rows), bf16),
        pltpu.VMEM((flat, rows), f32),
        pltpu.VMEM((32, rows), f32),
        pltpu.VMEM((32, rows), f32),
    )
    passed = pl.pallas_call(
        functools.partial(exchange, n_dom, n_ens, scale),
        out_shape=fields,
        in_specs=[hbm] * 9,
        out_specs=(vmem,) * len(fields),
        scratch_shapes=[
            pltpu.SMEM(class_kappa.shape, f32),
            pltpu.VMEM((32, rows), i32),
            pltpu.VMEM((flat, rows), bf16),
            pltpu.VMEM((flat, rows), f32),
            pltpu.VMEM((strips, flat, LANES), f32),
            pltpu.VMEM((flat, rows), f32),
            pltpu.VMEM((3, 1, count), i32),
            pltpu.VMEM((3, 1, count), f32),
            pltpu.VMEM((3, 1, count), f32),
            pltpu.VMEM((strips, 64, LANES), f32),
            eight,
            eight,
            pltpu.VMEM((count // HALF, groups, 2, HALF), f32),
            pltpu.VMEM((2, count // HALF, groups, 2, HALF), f32),
            pltpu.VMEM((PASSES + 1, 19, tall, rows), f32),
            pltpu.VMEM((n_ens, 4, 8, rows), f32),
            eight,
            pltpu.VMEM((n_ens, 8, 8, rows), f32),
            eight, eight, eight,
            pltpu.VMEM((3, HALF, count), bf16),
            pltpu.VMEM((flat, count), bf16),
            dma((9,)), dma((2, 3)), dma((2, 3)),
            dma((2,)), dma((2,)), dma((2,)), dma((2,)),
            dma((2, count // HALF // 2)), dma((2, count // HALF // 2)),
            dma((n_ens,)), dma((n_ens,)),
            dma((2,)), dma((2,)),
            dma((2, n_ens)), dma((2, n_ens)), dma((2, n_ens)), dma((2, n_ens)),
        ],
        compiler_params=pltpu.CompilerParams(
            collective_id=0, has_side_effects=True, vmem_limit_bytes=60 * 2**20
        ),
        name="exchange",
    )(
        class_kappa, alpha.reshape(flat, rows), perturb.reshape(flat, rows),
        static_ctl.reshape(32, rows), sigma.reshape(32, rows), class_index.reshape(32, rows),
        obs_cell.reshape(1, count), obs_value.reshape(1, count), obs_weight.reshape(1, count),
    )
    ga, gs = pl.pallas_call(
        functools.partial(adjoint, scale),
        out_shape=(
            jax.ShapeDtypeStruct((flat, rows), f32),
            jax.ShapeDtypeStruct((32, rows), f32),
        ),
        in_specs=[vmem] * len(fields),
        out_specs=(hbm,) * 2,
        scratch_shapes=[
            pltpu.VMEM((flat, rows), f32),
            pltpu.VMEM((strips, flat, LANES), f32),
            pltpu.VMEM((strips, 32, LANES), f32),
            pltpu.VMEM((32, rows), f32),
            pltpu.VMEM((19, tall, rows), f32),
            dma((2,)), dma(()),
        ],
        compiler_params=pltpu.CompilerParams(vmem_limit_bytes=24 * 2**20),
        name="adjoint",
    )(*passed)
    return ga.reshape(alpha.shape), gs.reshape(static_ctl.shape)


def solution(mesh):
    return jax.shard_map(
        per_device,
        mesh=mesh,
        in_specs=(
            P("ens", None, "dom", None),
            P("ens", None, "dom", None),
            P(None, "dom", None),
            P(None, "dom", None),
            P(None, "dom", None),
            P(),
            P("dom"),
            P("dom"),
            P("dom"),
        ),
        out_specs=(P("ens", None, "dom", None), P(None, "dom", None)),
        check_vma=False,
    )
```

```python
import functools
import math

import jax
import jax.numpy as jnp
from jax import lax
from jax.experimental import pallas as pl
from jax.experimental.pallas import tpu as pltpu
from jax.sharding import PartitionSpec as P

PASSES = 4
MESH = pl.DeviceIdType.MESH
LANES = 128
HALF = 256
PIECES = 3
CHUNKS = 4
f32 = jnp.float32
bf16 = jnp.bfloat16


def sub(shape):
    return lax.broadcasted_iota(jnp.int32, shape, len(shape) - 2)


def low_rows(shape):
    return sub(shape) < 4


def flip(x):
    return pltpu.roll(x, 4, 0)


def pair(a, b):
    return jnp.where(low_rows(a.shape), a, b)


def spread(x):
    other, low = flip(x), low_rows(x.shape)
    return jnp.where(low, x, other), jnp.where(low, other, x)


def march(old, new, fx, fy, wrap, first, quads):
    groups = old.shape[1] // 8
    strips = fx.shape[-1] // LANES

    def get(ref, c, g=0):
        return [ref[c, 8 * g : 8 * g + 8, block(v)] for v in range(strips)]

    def body(i, left):
        c0 = first + 1 + 4 * i
        us = [[get(old, c0 + k, g) for g in range(groups)] for k in range(5)]
        after = [[pltpu.roll(us[k][g][0], LANES - 1, 1) for g in range(groups)] for k in range(4)]
        before = [[pltpu.roll(us[k][g][-1], 1, 1) for g in range(groups)] for k in range(4)]
        out = []
        for k in range(4):
            face, side, first_side = get(fx, c0 + k), get(fy, c0 + k), wrap[c0 + k]
            fluxes = []
            for g in range(groups):
                u, there = us[k][g], us[k + 1][g]
                right = [f * (b - a) for f, a, b in zip(face, u, there, strict=True)]
                up = [f * (b - a) for f, a, b in zip(side, u, u[1:] + [after[k][g]], strict=True)]
                down = [first_side * (u[0] - before[k][g])] + up[:-1]
                out.append([
                    a + (x - y) + (p - q)
                    for a, x, y, p, q in zip(u, right, left[g], up, down, strict=True)
                ])
                fluxes.append(right)
            left = fluxes
        for k in range(4):
            for g in range(groups):
                for v in range(strips):
                    new[c0 + k, 8 * g : 8 * g + 8, block(v)] = out[k * groups + g][v]
        return left

    start = [
        [f * (b - a) for f, a, b in zip(get(fx, first), get(old, first, g), get(old, first + 1, g), strict=True)]
        for g in range(groups)
    ]
    lax.fori_loop(0, quads, body, start)


def spot(cell):
    return (cell & -512) | ((cell & 3) << 7) | ((cell & 511) >> 2)


def order_rows(x, order):
    pieces = [piece.astype(bf16) for piece in split3(x)]
    return sum(jnp.dot(piece, order[...], preferred_element_type=f32) for piece in reversed(pieces))


def natural_rows(x, order):
    high = x.astype(bf16)
    low = (x - high.astype(f32)).astype(bf16)
    dims = (((1,), (1,)), ((), ()))
    return lax.dot_general(low, order[...], dims, preferred_element_type=f32) + lax.dot_general(
        high, order[...], dims, preferred_element_type=f32
    )


def split3(x):
    out = []
    for _ in range(PIECES):
        out.append(x.astype(bf16).astype(f32))
        x = x - out[-1]
    return out


def block(v):
    return slice(v * LANES, (v + 1) * LANES)


def take(ref, at, count=8):
    return jnp.concatenate(
        [ref[v, pl.ds(at, count, stride=8), :] for v in range(ref.shape[0])], axis=1
    )


def put(ref, at, value):
    for v in range(ref.shape[0]):
        ref[v, pl.ds(at, value.shape[0], stride=8), :] = value[:, block(v)]


def lanes_of(t):
    return pl.ds(pl.multiple_of(t * LANES, LANES), LANES)


def hot_rows(cell, hot, t):
    low = (cell & (HALF - 1)).astype(f32)
    spot = lax.broadcasted_iota(jnp.int32, (HALF, LANES), 0).astype(f32)
    hot[:, lanes_of(t)] = jnp.where(spot == low, 1.0, 0.0).astype(bf16)


def exchange(
    n_dom, n_ens, scale,
    kappa_in, alpha_in, perturb_in, static_in, sigma_in, index_in, cell_in, value_in, weight_in,
    adj, member, fx, fy, wrap, order, alpha, static, sigma,
    kappa, index, perturb, ordered, wide, natural, cells, values, weights, twice, edge, known, p_send, p_recv,
    field, shared, plain, tails, w_all, v_all, n_all, hot, x_all,
    in_sem, o_ss, o_rs, c_ss, c_rs, k_ss, k_rs, p_ss, p_rs, s_ss, s_rs, i_ss, i_rs, t_ss, t_rs, m_ss, m_rs,
):
    me, ens = lax.axis_index("dom"), lax.axis_index("ens")
    right, left = lax.rem(me + 1, n_dom), lax.rem(me + n_dom - 1, n_dom)
    rows = fx.shape[-1]
    strips = rows // LANES
    groups = member.shape[1] // 8
    deep = cells.shape[-1] // HALF
    sides = ((0, left), (1, right))

    barrier = pltpu.get_barrier_semaphore()
    for side in (left, right):
        for r in range(n_ens):
            pl.semaphore_signal(
                barrier, inc=1, device_id=(side, lax.rem(ens + r, n_ens)), device_id_type=MESH
            )
    for r in range(1, n_ens):
        pl.semaphore_signal(
            barrier, inc=1, device_id=(me, lax.rem(ens + r, n_ens)), device_id_type=MESH
        )

    loads = [
        pltpu.make_async_copy(src, dst, in_sem.at[i])
        for i, (src, dst) in enumerate((
            (index_in, index), (kappa_in, kappa), (cell_in, cells.at[2]), (perturb_in, perturb),
            (static_in, static), (sigma_in, sigma), (weight_in, weights.at[2]), (value_in, values.at[2]),
            (alpha_in, alpha),
        ))
    ]
    for copy in loads:
        copy.start()

    def remote(src, dst, ss, rs, side, r=0):
        return pltpu.make_async_remote_copy(
            src_ref=src, dst_ref=dst, send_sem=ss, recv_sem=rs,
            device_id=(side, lax.rem(ens + r, n_ens)), device_id_type=MESH,
        )

    def started(copies):
        for copy in copies:
            copy.start()
        return copies

    def swap(ref, ss, rs):
        return [
            remote(ref.at[pl.ds(2 + 2 * s, 2)], ref.at[pl.ds(6 - 6 * s, 2)], ss.at[s], rs.at[1 - s], side)
            for s, side in sides
        ]

    def pairs_of(value, out):
        for v in range(strips):
            for level in range(4):
                tile = value(level, v)
                twice[v, 8 * level : 8 * level + 8, :] = tile
                twice[v, 32 + 8 * level : 40 + 8 * level, :] = tile
        for v in range(strips):
            for j in range(4):
                a, b = [twice[v, pl.ds(2 * j + i, 8, stride=8), :] for i in range(2)]
                out[2 + j, :, block(v)] = pair(a, b)

    zero = jnp.zeros((8, rows), f32)

    def sort_rows(v, carry):
        row = lax.broadcasted_iota(jnp.int32, (LANES, rows), 0) + v * LANES
        to = ((row & 3) << 7) | (row >> 2)
        here = lax.broadcasted_iota(jnp.int32, (LANES, rows), 1)
        order[pl.ds(pl.multiple_of(v * LANES, LANES), LANES), :] = jnp.where(to == here, 1.0, 0.0).astype(bf16)
        return carry

    lax.fori_loop(0, strips, sort_rows, 0)

    def clear(g, carry):
        at = pl.ds(pl.multiple_of(8 * g, 8), 8)
        for p, outer in ((0, (3, 4, 13, 14, 15, 16)), (1, (2, 3)), (2, (1, 2, 15, 16, 17, 18)), (3, (0, 1))):
            for c in outer:
                field[p, c, at] = zero
        return carry

    lax.fori_loop(0, groups, clear, 0)

    loads[0].wait()
    loads[1].wait()
    number = jnp.dot(index[...].astype(f32).astype(bf16), order[...], preferred_element_type=f32)

    def coefficient(level, v):
        mine = number[8 * level : 8 * level + 8, block(v)]
        out = jnp.zeros((8, LANES), f32)
        for k in range(kappa.shape[0]):
            out = jnp.where(mine == k, kappa[k], out)
        return out

    pairs_of(coefficient, edge)

    def pass_on(src, dst, i):
        return [remote(src, dst.at[1 - s], o_ss.at[s, i], o_rs.at[1 - s, i], side) for s, side in sides]

    edge_copies = swap(edge, c_ss, c_rs)
    first_copies = edge_copies + pass_on(cell_in, cells, 0)

    def greet(now):
        @pl.when(now)
        def _():
            pl.semaphore_wait(barrier, 3 * n_ens - 1)
            for copy in first_copies:
                copy.start()

    greet(me != 0)
    loads[3].wait()
    ordered[...] = jnp.dot(perturb[...], order[...], preferred_element_type=f32)
    perturb[...] = ordered[...].astype(bf16)
    loads[2].wait()

    def collect(n, carry):
        for i in range(4):
            hot_rows(spot(cells[2, :, lanes_of(4 * n + i)]), hot.at[2], 4 * n + i)
        span = pl.ds(pl.multiple_of(n * 2 * HALF, 2 * HALF), 2 * HALF)
        found = [
            lax.dot_general(
                perturb[:, h * HALF : (h + 1) * HALF], hot[2, :, span],
                (((1,), (0,)), ((), ())), preferred_element_type=f32,
            )
            for h in range(2)
        ]
        column = sub((8, LANES)) * 2
        for i in range(4):
            key = lax.shift_right_logical(spot(cells[2, :, lanes_of(4 * n + i)]), 8)
            masks = [[column + (16 * level + h) == key for h in range(2)] for level in range(4)]
            for m in range(2 * groups):
                kept = jnp.zeros((8, LANES), f32)
                for level in range(4):
                    for h in range(2):
                        at = (m * 4 + level) * 8
                        piece = found[h][at : at + 8, block(i)]
                        kept = jnp.where(masks[level][h], piece, kept)
                p_send[2 * n + i // 2, m // 2, m % 2 : m % 2 + 1, block(i % 2)] = jnp.sum(
                    kept, axis=0, keepdims=True
                )
        return carry

    def p_copy(s, side, n):
        part = pl.ds(2 * n, 2)
        return remote(p_send.at[part], p_recv.at[1 - s, part], p_ss.at[s, n], p_rs.at[1 - s, n], side)

    def collect_and_send(n, carry):
        collect(n, carry)

        @pl.when(me != 0)
        def _():
            started([p_copy(s, side, n) for s, side in sides])

        return carry

    lax.fori_loop(0, deep // 2, collect_and_send, 0)

    greet(me == 0)
    pl.when(me == 0)(lambda: started([p_copy(0, left, n) for n in range(deep // 2)]) and None)

    loads[4].wait()
    loads[5].wait()
    product = order_rows(static[...] * sigma[...], order)
    pairs_of(lambda level, v: product[8 * level : 8 * level + 8, block(v)], known)
    pl.when(me == 0)(lambda: started([p_copy(1, right, n) for n in range(deep // 2)]) and None)

    for v in range(strips):
        wide[v] = ordered[:, block(v)]

    def arrange(ref, at):
        def column(c, carry):
            for g in range(groups):
                ref[at + c, 8 * g : 8 * g + 8] = take(wide, g * 64 + c)
            return carry

        lax.fori_loop(0, 8, column, 0)

    arrange(member, 4)
    loads[8].wait()
    natural[...] = order_rows(alpha[...], order)
    for v in range(strips):
        wide[v] = natural[:, block(v)]
    arrange(field.at[0], 5)

    column_pairs = (sub((8, LANES)) % 4) * 16 + (sub((8, LANES)) // 4) * 2

    def weigh(q, carry):
        slot = jnp.where(q == 0, 0, jnp.where(q == 3, 1, 2))
        first = 2 * (1 - q % 2)

        def fill(t, carry):
            at = lanes_of(t)
            key = lax.shift_right_logical(spot(cells[slot, :, at]), 8)
            weight = weights[slot, :, at]
            pieces = split3(weight) + split3(weight * values[slot, :, at]) + [jnp.ones_like(weight)]
            masks = [column_pairs + (4 * (first + n) + h) == key for h in range(2) for n in range(2)]
            out = [jnp.where(mask, piece, 0.0) for piece in pieces for mask in masks]
            x_all[0 : 8 * len(out), at] = jnp.concatenate(out, axis=0).astype(bf16)
            return carry

        lax.fori_loop(0, 2 * deep, fill, 0)
        sums = lax.dot_general(
            x_all[0 : 7 * 32, :], hot[slot], (((1,), (1,)), ((), ())), preferred_element_type=f32
        )
        part = [sums[i * 32 : (i + 1) * 32] for i in range(7)]
        for ref, value in (
            (w_all, (part[2] + part[1]) + part[0]), (v_all, (part[5] + part[4]) + part[3]), (n_all, part[6])
        ):
            for h in range(2):
                for n in range(2):
                    row = (h * 2 + n) * 8
                    ref[2 * q + n, :, h * HALF : (h + 1) * HALF] = value[row : row + 8]
        return carry


    lane = lax.broadcasted_iota(jnp.int32, (8, LANES), 1)

    def faces(j, previous):
        for i, here in enumerate(spread(edge[j])):
            c = 2 * j + i
            blocks = [here[:, block(v)] for v in range(strips)]
            after = blocks[1:] + [pltpu.roll(blocks[0], LANES - 1, 1)]
            up = [0.5 * (a + b) for a, b in zip(blocks, after, strict=True)]
            up[-1] = jnp.where(lane < LANES - 1, up[-1], 0.0)
            for v in range(strips):
                fy[c + 1, :, block(v)] = up[v]
            wrap[c + 1] = pltpu.roll(up[-1], 1, 1)
            fx[c] = 0.5 * (previous + here)
            previous = here
        return previous


    def forward(p, carry):
        march(field.at[p], field.at[p + 1], fx, fy, wrap, 3 - p, 2)
        return carry

    def forward_right(p, carry):
        march(field.at[p], field.at[p + 1], fx, fy, wrap, 11 - p, 1 + p // 2)
        return carry

    def both(x):
        return x + flip(x)

    def gather(j):
        sums = []
        for i in range(2):
            c = 2 * j + i
            acc = member[c, 0:8] * field[PASSES, c + 1, 0:8]
            for g in range(1, groups):
                acc = acc + member[c, 8 * g : 8 * g + 8] * field[PASSES, c + 1, 8 * g : 8 * g + 8]
            sums.append(both(acc))
        return pair(*sums)

    def inner(j, carry):
        shared[0, j] = gather(j + 2)
        return carry

    own_copies = [
        remote(shared.at[0], shared.at[r], s_ss.at[r], s_rs.at[r], me, r) for r in range(1, n_ens)
    ]

    def spread_left():
        edge_copies[1].wait()
        lax.fori_loop(0, 6, faces, zero)
        fx[0] = zero
        lax.fori_loop(0, PASSES, forward, 0)

    def spread_right():
        edge_copies[0].wait()
        lax.fori_loop(6, 8, faces, spread(edge[5])[1])
        fx[16], fx[17], fy[17], wrap[17] = zero, zero, zero, zero[:, block(0)]
        lax.fori_loop(0, PASSES, forward_right, 0)
        lax.fori_loop(0, 4, inner, 0)
        started(own_copies)

    level_of = (sub((8, LANES)) % 4) * 16
    upper = sub((8, LANES)) < 4

    def tail_copies(s, side):
        return [
            pltpu.make_async_remote_copy(
                src_ref=tails.at[0, pl.ds(6 * s, 2)], dst_ref=tails.at[r, pl.ds(4 - 2 * s, 2)],
                send_sem=t_ss.at[s, r], recv_sem=t_rs.at[1 - s, r],
                device_id=(side, lax.rem(ens + r, n_ens)), device_id_type=MESH,
            )
            for r in range(n_ens)
        ] + [
            pltpu.make_async_remote_copy(
                src_ref=tails.at[0, pl.ds(6 * s, 2)], dst_ref=tails.at[r, pl.ds(6 * s, 2)],
                send_sem=m_ss.at[s, r], recv_sem=m_rs.at[s, r],
                device_id=(me, lax.rem(ens + r, n_ens)), device_id_type=MESH,
            )
            for r in range(1, n_ens)
        ]

    plain_copies = swap(plain, i_ss, i_rs)

    def settle():
        for copy in own_copies:
            copy.wait()
        for j in range(4):
            whole = shared[lax.rem(ens + n_ens, n_ens), j]
            for e in range(1, n_ens):
                whole = whole + shared[lax.rem(ens - e + n_ens, n_ens), j]
            plain[2 + j] = whole
        started(plain_copies)

    final = me == n_dom - 1

    def beside(s, i):
        away = jnp.where(s == 0, right, left)
        remote(cell_in, cells.at[s], o_ss.at[1 - s, 0], o_rs.at[s, 0], away).wait()

        def place(t, carry):
            cell = spot(cells[s, :, lanes_of(t)])
            hot_rows(cell, hot.at[s], t)
            key = lax.shift_right_logical(cell, 8)
            at = lanes_of(t % 2)
            value = [
                jnp.where(upper, p_recv[s, t // 2, g, 0:1, at], p_recv[s, t // 2, g, 1:2, at])
                for g in range(groups)
            ]
            out = []
            for h in range(2):
                for c in range(4):
                    mask = level_of + (2 * (c + 4 - 4 * s) + h) == key
                    out += [jnp.where(mask, v, 0.0) for v in value]
            x_all[:, lanes_of(t)] = jnp.concatenate(out, axis=0).astype(bf16)
            return carry

        def part(n, carry):
            p_copy(1 - s, away, n).wait()
            return lax.fori_loop(4 * n, 4 * n + 4, place, carry)

        lax.fori_loop(0, deep // 2, part, 0)
        pl.when(i == jnp.where(final, 2, 1))(settle)
        found = lax.dot_general(
            x_all[...], hot[s], (((1,), (1,)), ((), ())), preferred_element_type=f32
        )
        for h in range(2):
            for c in range(4):
                for g in range(groups):
                    at = ((h * 4 + c) * groups + g) * 8
                    member[12 * s + c, 8 * g : 8 * g + 8, h * HALF : (h + 1) * HALF] = found[at : at + 8]


    def phase(i, carry):
        stencil = i == jnp.where(final, 1, 0)
        s = jnp.where(final, i // 2, jnp.where(me < 2, 2 - i, i - 1))
        pl.when(stencil)(spread_right)
        pl.when(jnp.logical_not(stencil))(lambda: beside(s, i))

        def tail(n, carry):
            out = jnp.where(final, 1 - n, s)
            for j in range(2):
                tails[0, 6 * out + j] = gather(6 * out + j)
            started(tail_copies(out, jnp.where(out == 0, left, right)))
            return carry

        lax.fori_loop(0, jnp.where(final, i // 2 * 2, jnp.minimum(i, 1)), tail, 0)
        return carry

    spread_left()
    weight_copies = started(pass_on(weight_in, weights, 1) + pass_on(value_in, values, 2))
    known_copies = started(swap(known, k_ss, k_rs))
    lax.fori_loop(0, 3, phase, 0)

    for copy in weight_copies:
        copy.wait()
    loads[6].wait()
    loads[7].wait()
    lax.fori_loop(0, 4, weigh, 0)

    for copy in known_copies + plain_copies + tail_copies(0, left) + tail_copies(1, right):
        copy.wait()

    def finish(j, carry):
        once = 1.0 / jnp.maximum(n_all[j], 1.0)
        whole = tails[lax.rem(ens + n_ens, n_ens), j]
        for e in range(1, n_ens):
            whole = whole + tails[lax.rem(ens - e + n_ens, n_ens), j]
        state = known[j] + scale * (plain[j] + whole * once)
        tile = w_all[j] * state - v_all[j]
        own = jnp.logical_and(j >= 2, j < 6)
        tile = jnp.where(own, tile, tile * once)
        adj[2 * j], adj[2 * j + 1] = spread(tile)
        return carry

    lax.fori_loop(0, 8, finish, 0)


def adjoint(
    scale, adj, member, fx, fy, wrap, order, alpha, static, sigma,
    ga, gs, out, wide, small, result, field, ga_sem, gs_sem,
):
    groups = member.shape[1] // 8
    strips = wide.shape[0]

    def begin(c, carry):
        one = adj[c]
        for g in range(groups):
            field[c + 1, 8 * g : 8 * g + 8] = member[c, 8 * g : 8 * g + 8] * one
        return carry

    lax.fori_loop(0, 16, begin, 0)

    def back(p, carry):
        march(field, field, fx, fy, wrap, p + 1, (17 - 2 * p) // 4)
        return carry

    lax.fori_loop(0, PASSES, back, 0)

    def end(c, carry):
        for g in range(groups):
            put(wide, g * 64 + c, field[5 + c, 8 * g : 8 * g + 8])
        put(small, c, adj[4 + c][0:4])
        return carry

    lax.fori_loop(0, 8, end, 0)

    def joined(ref, at):
        return jnp.concatenate([ref[v, at] for v in range(strips)], axis=1)

    part = 32 * groups
    copies = []
    for i in range(2):
        at = pl.ds(i * part, part)
        out[at] = alpha[at] + scale * natural_rows(joined(wide, at), order)
        copies.append(pltpu.make_async_copy(out.at[at], ga.at[at], ga_sem.at[i]))
        copies[-1].start()
    result[...] = static[...] + sigma[...] * natural_rows(joined(small, slice(None)), order)
    copies.append(pltpu.make_async_copy(result, gs, gs_sem))
    copies[-1].start()
    for copy in copies:
        copy.wait()


def per_device(
    alpha, perturb, static_ctl, sigma, class_index, class_kappa, obs_cell, obs_value, obs_weight
):
    n_dom, n_ens = lax.axis_size("dom"), lax.axis_size("ens")
    local, levels, columns, rows = alpha.shape
    assert columns == 8 and levels == 4 and rows == 512 and local % 2 == 0
    scale = 1.0 / math.sqrt(local * n_ens - 1)
    count = obs_cell.shape[0]
    groups = local // 2
    flat = local * 32
    tall = groups * 8
    strips = rows // LANES
    hbm = pl.BlockSpec(memory_space=pltpu.HBM)
    vmem = pl.BlockSpec(memory_space=pltpu.VMEM)
    dma = pltpu.SemaphoreType.DMA
    i32 = jnp.int32
    eight = pltpu.VMEM((8, 8, rows), f32)
    fields = (
        pltpu.VMEM((16, 8, rows), f32),
        pltpu.VMEM((16, tall, rows), f32),
        pltpu.VMEM((18, 8, rows), f32),
        pltpu.VMEM((18, 8, rows), f32),
        pltpu.VMEM((18, 8, LANES), f32),
        pltpu.VMEM((rows, rows), bf16),
        pltpu.VMEM((flat, rows), f32),
        pltpu.VMEM((32, rows), f32),
        pltpu.VMEM((32, rows), f32),
    )
    passed = pl.pallas_call(
        functools.partial(exchange, n_dom, n_ens, scale),
        out_shape=fields,
        in_specs=[hbm] * 9,
        out_specs=(vmem,) * len(fields),
        scratch_shapes=[
            pltpu.SMEM(class_kappa.shape, f32),
            pltpu.VMEM((32, rows), i32),
            pltpu.VMEM((flat, rows), bf16),
            pltpu.VMEM((flat, rows), f32),
            pltpu.VMEM((strips, flat, LANES), f32),
            pltpu.VMEM((flat, rows), f32),
            pltpu.VMEM((3, 1, count), i32),
            pltpu.VMEM((3, 1, count), f32),
            pltpu.VMEM((3, 1, count), f32),
            pltpu.VMEM((strips, 64, LANES), f32),
            eight,
            eight,
            pltpu.VMEM((count // HALF, groups, 2, HALF), f32),
            pltpu.VMEM((2, count // HALF, groups, 2, HALF), f32),
            pltpu.VMEM((PASSES + 1, 19, tall, rows), f32),
            pltpu.VMEM((n_ens, 4, 8, rows), f32),
            eight,
            pltpu.VMEM((n_ens, 8, 8, rows), f32),
            eight, eight, eight,
            pltpu.VMEM((3, HALF, count), bf16),
            pltpu.VMEM((flat, count), bf16),
            dma((9,)), dma((2, 3)), dma((2, 3)),
            dma((2,)), dma((2,)), dma((2,)), dma((2,)),
            dma((2, count // HALF // 2)), dma((2, count // HALF // 2)),
            dma((n_ens,)), dma((n_ens,)),
            dma((2,)), dma((2,)),
            dma((2, n_ens)), dma((2, n_ens)), dma((2, n_ens)), dma((2, n_ens)),
        ],
        compiler_params=pltpu.CompilerParams(
            collective_id=0, has_side_effects=True, vmem_limit_bytes=60 * 2**20
        ),
        name="exchange",
    )(
        class_kappa, alpha.reshape(flat, rows), perturb.reshape(flat, rows),
        static_ctl.reshape(32, rows), sigma.reshape(32, rows), class_index.reshape(32, rows),
        obs_cell.reshape(1, count), obs_value.reshape(1, count), obs_weight.reshape(1, count),
    )
    ga, gs = pl.pallas_call(
        functools.partial(adjoint, scale),
        out_shape=(
            jax.ShapeDtypeStruct((flat, rows), f32),
            jax.ShapeDtypeStruct((32, rows), f32),
        ),
        in_specs=[vmem] * len(fields),
        out_specs=(hbm,) * 2,
        scratch_shapes=[
            pltpu.VMEM((flat, rows), f32),
            pltpu.VMEM((strips, flat, LANES), f32),
            pltpu.VMEM((strips, 32, LANES), f32),
            pltpu.VMEM((32, rows), f32),
            pltpu.VMEM((19, tall, rows), f32),
            dma((2,)), dma(()),
        ],
        compiler_params=pltpu.CompilerParams(vmem_limit_bytes=24 * 2**20),
        name="adjoint",
    )(*passed)
    return ga.reshape(alpha.shape), gs.reshape(static_ctl.shape)


def solution(mesh):
    return jax.shard_map(
        per_device,
        mesh=mesh,
        in_specs=(
            P("ens", None, "dom", None),
            P("ens", None, "dom", None),
            P(None, "dom", None),
            P(None, "dom", None),
            P(None, "dom", None),
            P(),
            P("dom"),
            P("dom"),
            P("dom"),
        ),
        out_specs=(P("ens", None, "dom", None), P(None, "dom", None)),
        check_vma=False,
    )
```

```python
import functools
import math

import jax
import jax.numpy as jnp
from jax import lax
from jax.experimental import pallas as pl
from jax.experimental.pallas import tpu as pltpu
from jax.sharding import PartitionSpec as P

PASSES = 4
MESH = pl.DeviceIdType.MESH
LANES = 128
HALF = 256
PIECES = 3
CHUNKS = 4
f32 = jnp.float32
bf16 = jnp.bfloat16


def sub(shape):
    return lax.broadcasted_iota(jnp.int32, shape, len(shape) - 2)


def low_rows(shape):
    return sub(shape) < 4


def flip(x):
    return pltpu.roll(x, 4, 0)


def pair(a, b):
    return jnp.where(low_rows(a.shape), a, b)


def spread(x):
    other, low = flip(x), low_rows(x.shape)
    return jnp.where(low, x, other), jnp.where(low, other, x)


def march(old, new, fx, fy, wrap, first, quads):
    groups = old.shape[1] // 8
    strips = fx.shape[-1] // LANES

    def get(ref, c, g=0):
        return [ref[c, 8 * g : 8 * g + 8, block(v)] for v in range(strips)]

    def body(i, left):
        c0 = first + 1 + 4 * i
        us = [[get(old, c0 + k, g) for g in range(groups)] for k in range(5)]
        after = [[pltpu.roll(us[k][g][0], LANES - 1, 1) for g in range(groups)] for k in range(4)]
        before = [[pltpu.roll(us[k][g][-1], 1, 1) for g in range(groups)] for k in range(4)]
        out = []
        for k in range(4):
            face, side, first_side = get(fx, c0 + k), get(fy, c0 + k), wrap[c0 + k]
            fluxes = []
            for g in range(groups):
                u, there = us[k][g], us[k + 1][g]
                right = [f * (b - a) for f, a, b in zip(face, u, there, strict=True)]
                up = [f * (b - a) for f, a, b in zip(side, u, u[1:] + [after[k][g]], strict=True)]
                down = [first_side * (u[0] - before[k][g])] + up[:-1]
                out.append([
                    a + (x - y) + (p - q)
                    for a, x, y, p, q in zip(u, right, left[g], up, down, strict=True)
                ])
                fluxes.append(right)
            left = fluxes
        for k in range(4):
            for g in range(groups):
                for v in range(strips):
                    new[c0 + k, 8 * g : 8 * g + 8, block(v)] = out[k * groups + g][v]
        return left

    start = [
        [f * (b - a) for f, a, b in zip(get(fx, first), get(old, first, g), get(old, first + 1, g), strict=True)]
        for g in range(groups)
    ]
    lax.fori_loop(0, quads, body, start)


def spot(cell):
    return (cell & -512) | ((cell & 3) << 7) | ((cell & 511) >> 2)


def order_rows(x, order):
    pieces = [piece.astype(bf16) for piece in split3(x)]
    every = jnp.dot(jnp.concatenate(pieces[::-1], axis=0), order[...], preferred_element_type=f32)
    n = x.shape[0]
    return (every[:n] + every[n : 2 * n]) + every[2 * n :]


def natural_rows(x, order):
    high = x.astype(bf16)
    low = (x - high.astype(f32)).astype(bf16)
    both = lax.dot_general(
        jnp.concatenate([low, high], axis=0), order[...], (((1,), (1,)), ((), ())), preferred_element_type=f32
    )
    return both[: x.shape[0]] + both[x.shape[0] :]


def split3(x):
    out = []
    for _ in range(PIECES):
        out.append(x.astype(bf16).astype(f32))
        x = x - out[-1]
    return out


def block(v):
    return slice(v * LANES, (v + 1) * LANES)


def take(ref, at, count=8):
    return jnp.concatenate(
        [ref[v, pl.ds(at, count, stride=8), :] for v in range(ref.shape[0])], axis=1
    )


def put(ref, at, value):
    for v in range(ref.shape[0]):
        ref[v, pl.ds(at, value.shape[0], stride=8), :] = value[:, block(v)]


def lanes_of(t):
    return pl.ds(pl.multiple_of(t * LANES, LANES), LANES)


def hot_rows(cell, hot, t):
    low = (cell & (HALF - 1)).astype(f32)
    spot = lax.broadcasted_iota(jnp.int32, (HALF, LANES), 0).astype(f32)
    hot[:, lanes_of(t)] = jnp.where(spot == low, 1.0, 0.0).astype(bf16)


def exchange(
    n_dom, n_ens, scale,
    kappa_in, alpha_in, perturb_in, static_in, sigma_in, index_in, cell_in, value_in, weight_in,
    adj, member, fx, fy, wrap, order, alpha, static, sigma,
    kappa, index, perturb, ordered, wide, natural, cells, values, weights, twice, edge, known, p_send, p_recv,
    field, shared, plain, tails, w_all, v_all, n_all, hot, x_all,
    in_sem, o_ss, o_rs, c_ss, c_rs, k_ss, k_rs, p_ss, p_rs, s_ss, s_rs, i_ss, i_rs, t_ss, t_rs, m_ss, m_rs,
):
    me, ens = lax.axis_index("dom"), lax.axis_index("ens")
    right, left = lax.rem(me + 1, n_dom), lax.rem(me + n_dom - 1, n_dom)
    rows = fx.shape[-1]
    strips = rows // LANES
    groups = member.shape[1] // 8
    deep = cells.shape[-1] // HALF
    sides = ((0, left), (1, right))

    barrier = pltpu.get_barrier_semaphore()
    for side in (left, right):
        for r in range(n_ens):
            pl.semaphore_signal(
                barrier, inc=1, device_id=(side, lax.rem(ens + r, n_ens)), device_id_type=MESH
            )
    for r in range(1, n_ens):
        pl.semaphore_signal(
            barrier, inc=1, device_id=(me, lax.rem(ens + r, n_ens)), device_id_type=MESH
        )

    loads = [
        pltpu.make_async_copy(src, dst, in_sem.at[i])
        for i, (src, dst) in enumerate((
            (index_in, index), (kappa_in, kappa), (cell_in, cells.at[2]), (perturb_in, perturb),
            (static_in, static), (sigma_in, sigma), (weight_in, weights.at[2]), (value_in, values.at[2]),
            (alpha_in, alpha),
        ))
    ]
    for copy in loads:
        copy.start()

    def remote(src, dst, ss, rs, side, r=0):
        return pltpu.make_async_remote_copy(
            src_ref=src, dst_ref=dst, send_sem=ss, recv_sem=rs,
            device_id=(side, lax.rem(ens + r, n_ens)), device_id_type=MESH,
        )

    def started(copies):
        for copy in copies:
            copy.start()
        return copies

    def swap(ref, ss, rs):
        return [
            remote(ref.at[pl.ds(2 + 2 * s, 2)], ref.at[pl.ds(6 - 6 * s, 2)], ss.at[s], rs.at[1 - s], side)
            for s, side in sides
        ]

    def pairs_of(value, out):
        for v in range(strips):
            for level in range(4):
                tile = value(level, v)
                twice[v, 8 * level : 8 * level + 8, :] = tile
                twice[v, 32 + 8 * level : 40 + 8 * level, :] = tile
        for v in range(strips):
            for j in range(4):
                a, b = [twice[v, pl.ds(2 * j + i, 8, stride=8), :] for i in range(2)]
                out[2 + j, :, block(v)] = pair(a, b)

    zero = jnp.zeros((8, rows), f32)

    def sort_rows(v, carry):
        row = lax.broadcasted_iota(jnp.int32, (LANES, rows), 0) + v * LANES
        to = ((row & 3) << 7) | (row >> 2)
        here = lax.broadcasted_iota(jnp.int32, (LANES, rows), 1)
        order[pl.ds(pl.multiple_of(v * LANES, LANES), LANES), :] = jnp.where(to == here, 1.0, 0.0).astype(bf16)
        return carry

    lax.fori_loop(0, strips, sort_rows, 0)

    def clear(g, carry):
        at = pl.ds(pl.multiple_of(8 * g, 8), 8)
        for p, outer in ((0, (3, 4, 13, 14, 15, 16)), (1, (2, 3)), (2, (1, 2, 15, 16, 17, 18)), (3, (0, 1))):
            for c in outer:
                field[p, c, at] = zero
        return carry

    lax.fori_loop(0, groups, clear, 0)

    loads[0].wait()
    loads[1].wait()
    number = jnp.dot(index[...].astype(f32).astype(bf16), order[...], preferred_element_type=f32)

    def coefficient(level, v):
        mine = number[8 * level : 8 * level + 8, block(v)]
        out = jnp.zeros((8, LANES), f32)
        for k in range(kappa.shape[0]):
            out = jnp.where(mine == k, kappa[k], out)
        return out

    pairs_of(coefficient, edge)

    def pass_on(src, dst, i):
        return [remote(src, dst.at[1 - s], o_ss.at[s, i], o_rs.at[1 - s, i], side) for s, side in sides]

    edge_copies = swap(edge, c_ss, c_rs)
    first_copies = edge_copies + pass_on(cell_in, cells, 0)

    def greet(now):
        @pl.when(now)
        def _():
            pl.semaphore_wait(barrier, 3 * n_ens - 1)
            for copy in first_copies:
                copy.start()

    greet(me != 0)
    loads[3].wait()
    ordered[...] = jnp.dot(perturb[...], order[...], preferred_element_type=f32)
    perturb[...] = ordered[...].astype(bf16)
    loads[2].wait()

    def collect(n, carry):
        for i in range(4):
            hot_rows(spot(cells[2, :, lanes_of(4 * n + i)]), hot.at[2], 4 * n + i)
        span = pl.ds(pl.multiple_of(n * 2 * HALF, 2 * HALF), 2 * HALF)
        found = [
            lax.dot_general(
                perturb[:, h * HALF : (h + 1) * HALF], hot[2, :, span],
                (((1,), (0,)), ((), ())), preferred_element_type=f32,
            )
            for h in range(2)
        ]
        column = sub((8, LANES)) * 2
        for i in range(4):
            key = lax.shift_right_logical(spot(cells[2, :, lanes_of(4 * n + i)]), 8)
            masks = [[column + (16 * level + h) == key for h in range(2)] for level in range(4)]
            for m in range(2 * groups):
                kept = jnp.zeros((8, LANES), f32)
                for level in range(4):
                    for h in range(2):
                        at = (m * 4 + level) * 8
                        piece = found[h][at : at + 8, block(i)]
                        kept = jnp.where(masks[level][h], piece, kept)
                p_send[2 * n + i // 2, m // 2, m % 2 : m % 2 + 1, block(i % 2)] = jnp.sum(
                    kept, axis=0, keepdims=True
                )
        return carry

    def p_copy(s, side, n):
        part = pl.ds(2 * n, 2)
        return remote(p_send.at[part], p_recv.at[1 - s, part], p_ss.at[s, n], p_rs.at[1 - s, n], side)

    def collect_and_send(n, carry):
        collect(n, carry)

        @pl.when(me != 0)
        def _():
            started([p_copy(s, side, n) for s, side in sides])

        return carry

    lax.fori_loop(0, deep // 2, collect_and_send, 0)

    greet(me == 0)
    pl.when(me == 0)(lambda: started([p_copy(0, left, n) for n in range(deep // 2)]) and None)

    loads[4].wait()
    loads[5].wait()
    product = order_rows(static[...] * sigma[...], order)
    pairs_of(lambda level, v: product[8 * level : 8 * level + 8, block(v)], known)
    pl.when(me == 0)(lambda: started([p_copy(1, right, n) for n in range(deep // 2)]) and None)

    for v in range(strips):
        wide[v] = ordered[:, block(v)]

    def arrange(ref, at):
        def column(c, carry):
            for g in range(groups):
                ref[at + c, 8 * g : 8 * g + 8] = take(wide, g * 64 + c)
            return carry

        lax.fori_loop(0, 8, column, 0)

    arrange(member, 4)
    loads[8].wait()
    natural[...] = order_rows(alpha[...], order)
    for v in range(strips):
        wide[v] = natural[:, block(v)]
    arrange(field.at[0], 5)

    column_pairs = (sub((8, LANES)) % 4) * 16 + (sub((8, LANES)) // 4) * 2

    def weigh(q, carry):
        slot = jnp.where(q == 0, 0, jnp.where(q == 3, 1, 2))
        first = 2 * (1 - q % 2)

        def fill(t, carry):
            at = lanes_of(t)
            key = lax.shift_right_logical(spot(cells[slot, :, at]), 8)
            weight = weights[slot, :, at]
            pieces = split3(weight) + split3(weight * values[slot, :, at]) + [jnp.ones_like(weight)]
            masks = [column_pairs + (4 * (first + n) + h) == key for h in range(2) for n in range(2)]
            out = [jnp.where(mask, piece, 0.0) for piece in pieces for mask in masks]
            x_all[0 : 8 * len(out), at] = jnp.concatenate(out, axis=0).astype(bf16)
            return carry

        lax.fori_loop(0, 2 * deep, fill, 0)
        sums = lax.dot_general(
            x_all[0 : 7 * 32, :], hot[slot], (((1,), (1,)), ((), ())), preferred_element_type=f32
        )
        part = [sums[i * 32 : (i + 1) * 32] for i in range(7)]
        for ref, value in (
            (w_all, (part[2] + part[1]) + part[0]), (v_all, (part[5] + part[4]) + part[3]), (n_all, part[6])
        ):
            for h in range(2):
                for n in range(2):
                    row = (h * 2 + n) * 8
                    ref[2 * q + n, :, h * HALF : (h + 1) * HALF] = value[row : row + 8]
        return carry


    lane = lax.broadcasted_iota(jnp.int32, (8, LANES), 1)

    def faces(j, previous):
        for i, here in enumerate(spread(edge[j])):
            c = 2 * j + i
            blocks = [here[:, block(v)] for v in range(strips)]
            after = blocks[1:] + [pltpu.roll(blocks[0], LANES - 1, 1)]
            up = [0.5 * (a + b) for a, b in zip(blocks, after, strict=True)]
            up[-1] = jnp.where(lane < LANES - 1, up[-1], 0.0)
            for v in range(strips):
                fy[c + 1, :, block(v)] = up[v]
            wrap[c + 1] = pltpu.roll(up[-1], 1, 1)
            fx[c] = 0.5 * (previous + here)
            previous = here
        return previous


    def forward(p, carry):
        march(field.at[p], field.at[p + 1], fx, fy, wrap, 3 - p, 2)
        return carry

    def forward_right(p, carry):
        march(field.at[p], field.at[p + 1], fx, fy, wrap, 11 - p, 1 + p // 2)
        return carry

    def both(x):
        return x + flip(x)

    def gather(j):
        sums = []
        for i in range(2):
            c = 2 * j + i
            acc = member[c, 0:8] * field[PASSES, c + 1, 0:8]
            for g in range(1, groups):
                acc = acc + member[c, 8 * g : 8 * g + 8] * field[PASSES, c + 1, 8 * g : 8 * g + 8]
            sums.append(both(acc))
        return pair(*sums)

    def inner(j, carry):
        shared[0, j] = gather(j + 2)
        return carry

    own_copies = [
        remote(shared.at[0], shared.at[r], s_ss.at[r], s_rs.at[r], me, r) for r in range(1, n_ens)
    ]

    def spread_left():
        edge_copies[1].wait()
        lax.fori_loop(0, 6, faces, zero)
        fx[0] = zero
        lax.fori_loop(0, PASSES, forward, 0)

    def spread_right():
        edge_copies[0].wait()
        lax.fori_loop(6, 8, faces, spread(edge[5])[1])
        fx[16], fx[17], fy[17], wrap[17] = zero, zero, zero, zero[:, block(0)]
        lax.fori_loop(0, PASSES, forward_right, 0)
        lax.fori_loop(0, 4, inner, 0)
        started(own_copies)

    level_of = (sub((8, LANES)) % 4) * 16
    upper = sub((8, LANES)) < 4

    def tail_copies(s, side):
        return [
            pltpu.make_async_remote_copy(
                src_ref=tails.at[0, pl.ds(6 * s, 2)], dst_ref=tails.at[r, pl.ds(4 - 2 * s, 2)],
                send_sem=t_ss.at[s, r], recv_sem=t_rs.at[1 - s, r],
                device_id=(side, lax.rem(ens + r, n_ens)), device_id_type=MESH,
            )
            for r in range(n_ens)
        ] + [
            pltpu.make_async_remote_copy(
                src_ref=tails.at[0, pl.ds(6 * s, 2)], dst_ref=tails.at[r, pl.ds(6 * s, 2)],
                send_sem=m_ss.at[s, r], recv_sem=m_rs.at[s, r],
                device_id=(me, lax.rem(ens + r, n_ens)), device_id_type=MESH,
            )
            for r in range(1, n_ens)
        ]

    plain_copies = swap(plain, i_ss, i_rs)

    def settle():
        for copy in own_copies:
            copy.wait()
        for j in range(4):
            whole = shared[lax.rem(ens + n_ens, n_ens), j]
            for e in range(1, n_ens):
                whole = whole + shared[lax.rem(ens - e + n_ens, n_ens), j]
            plain[2 + j] = whole
        started(plain_copies)

    final = me == n_dom - 1

    def beside(s, i):
        away = jnp.where(s == 0, right, left)
        remote(cell_in, cells.at[s], o_ss.at[1 - s, 0], o_rs.at[s, 0], away).wait()

        def place(t, carry):
            cell = spot(cells[s, :, lanes_of(t)])
            hot_rows(cell, hot.at[s], t)
            key = lax.shift_right_logical(cell, 8)
            at = lanes_of(t % 2)
            value = [
                jnp.where(upper, p_recv[s, t // 2, g, 0:1, at], p_recv[s, t // 2, g, 1:2, at])
                for g in range(groups)
            ]
            out = []
            for h in range(2):
                for c in range(4):
                    mask = level_of + (2 * (c + 4 - 4 * s) + h) == key
                    out += [jnp.where(mask, v, 0.0) for v in value]
            x_all[:, lanes_of(t)] = jnp.concatenate(out, axis=0).astype(bf16)
            return carry

        def part(n, carry):
            p_copy(1 - s, away, n).wait()
            return lax.fori_loop(4 * n, 4 * n + 4, place, carry)

        lax.fori_loop(0, deep // 2, part, 0)
        pl.when(i == jnp.where(final, 2, 1))(settle)
        found = lax.dot_general(
            x_all[...], hot[s], (((1,), (1,)), ((), ())), preferred_element_type=f32
        )
        for h in range(2):
            for c in range(4):
                for g in range(groups):
                    at = ((h * 4 + c) * groups + g) * 8
                    member[12 * s + c, 8 * g : 8 * g + 8, h * HALF : (h + 1) * HALF] = found[at : at + 8]


    def weights_of(own):
        @pl.when(jnp.logical_not(own))
        def _():
            for copy in weight_copies:
                copy.wait()

        lax.fori_loop(0, 2, lambda n, carry: weigh(jnp.where(own, 1 + n, 3 * n), carry), 0)

    def phase(step, carry):
        i = step - jnp.where(me == 0, 1, 0)
        working = jnp.logical_and(i >= 0, i < 3)
        pl.when(jnp.logical_not(working))(lambda: weights_of(step == jnp.where(me == 0, 0, 3)))
        pl.when(working)(lambda: sided(i))
        return carry

    def sided(i):
        stencil = i == jnp.where(final, 1, 0)
        s = jnp.where(final, i // 2, jnp.where(me < 2, 2 - i, i - 1))
        pl.when(stencil)(spread_right)
        pl.when(jnp.logical_not(stencil))(lambda: beside(s, i))

        def tail(n, carry):
            out = jnp.where(final, 1 - n, s)
            for j in range(2):
                tails[0, 6 * out + j] = gather(6 * out + j)
            started(tail_copies(out, jnp.where(out == 0, left, right)))
            return carry

        lax.fori_loop(0, jnp.where(final, i // 2 * 2, jnp.minimum(i, 1)), tail, 0)

    loads[6].wait()
    loads[7].wait()
    spread_left()
    weight_copies = started(pass_on(weight_in, weights, 1) + pass_on(value_in, values, 2))
    known_copies = started(swap(known, k_ss, k_rs))
    lax.fori_loop(0, 5, phase, 0)

    for copy in known_copies + plain_copies + tail_copies(0, left) + tail_copies(1, right):
        copy.wait()

    def finish(j, carry):
        once = 1.0 / jnp.maximum(n_all[j], 1.0)
        whole = tails[lax.rem(ens + n_ens, n_ens), j]
        for e in range(1, n_ens):
            whole = whole + tails[lax.rem(ens - e + n_ens, n_ens), j]
        state = known[j] + scale * (plain[j] + whole * once)
        tile = w_all[j] * state - v_all[j]
        own = jnp.logical_and(j >= 2, j < 6)
        tile = jnp.where(own, tile, tile * once)
        adj[2 * j], adj[2 * j + 1] = spread(tile)
        return carry

    lax.fori_loop(0, 8, finish, 0)


def adjoint(
    scale, adj, member, fx, fy, wrap, order, alpha, static, sigma,
    ga, gs, out, wide, small, result, field, ga_sem, gs_sem,
):
    groups = member.shape[1] // 8
    strips = wide.shape[0]

    def begin(c, carry):
        one = adj[c]
        for g in range(groups):
            field[c + 1, 8 * g : 8 * g + 8] = member[c, 8 * g : 8 * g + 8] * one
        return carry

    lax.fori_loop(0, 16, begin, 0)

    def back(p, carry):
        march(field, field, fx, fy, wrap, p + 1, (17 - 2 * p) // 4)
        return carry

    lax.fori_loop(0, PASSES, back, 0)

    def end(c, carry):
        for g in range(groups):
            put(wide, g * 64 + c, field[5 + c, 8 * g : 8 * g + 8])
        put(small, c, adj[4 + c][0:4])
        return carry

    lax.fori_loop(0, 8, end, 0)

    def joined(ref, at):
        return jnp.concatenate([ref[v, at] for v in range(strips)], axis=1)

    part = 32 * groups
    copies = []
    for i in range(2):
        at = pl.ds(i * part, part)
        out[at] = alpha[at] + scale * natural_rows(joined(wide, at), order)
        copies.append(pltpu.make_async_copy(out.at[at], ga.at[at], ga_sem.at[i]))
        copies[-1].start()
    result[...] = static[...] + sigma[...] * natural_rows(joined(small, slice(None)), order)
    copies.append(pltpu.make_async_copy(result, gs, gs_sem))
    copies[-1].start()
    for copy in copies:
        copy.wait()


def per_device(
    alpha, perturb, static_ctl, sigma, class_index, class_kappa, obs_cell, obs_value, obs_weight
):
    n_dom, n_ens = lax.axis_size("dom"), lax.axis_size("ens")
    local, levels, columns, rows = alpha.shape
    assert columns == 8 and levels == 4 and rows == 512 and local % 2 == 0
    scale = 1.0 / math.sqrt(local * n_ens - 1)
    count = obs_cell.shape[0]
    groups = local // 2
    flat = local * 32
    tall = groups * 8
    strips = rows // LANES
    hbm = pl.BlockSpec(memory_space=pltpu.HBM)
    vmem = pl.BlockSpec(memory_space=pltpu.VMEM)
    dma = pltpu.SemaphoreType.DMA
    i32 = jnp.int32
    eight = pltpu.VMEM((8, 8, rows), f32)
    fields = (
        pltpu.VMEM((16, 8, rows), f32),
        pltpu.VMEM((16, tall, rows), f32),
        pltpu.VMEM((18, 8, rows), f32),
        pltpu.VMEM((18, 8, rows), f32),
        pltpu.VMEM((18, 8, LANES), f32),
        pltpu.VMEM((rows, rows), bf16),
        pltpu.VMEM((flat, rows), f32),
        pltpu.VMEM((32, rows), f32),
        pltpu.VMEM((32, rows), f32),
    )
    passed = pl.pallas_call(
        functools.partial(exchange, n_dom, n_ens, scale),
        out_shape=fields,
        in_specs=[hbm] * 9,
        out_specs=(vmem,) * len(fields),
        scratch_shapes=[
            pltpu.SMEM(class_kappa.shape, f32),
            pltpu.VMEM((32, rows), i32),
            pltpu.VMEM((flat, rows), bf16),
            pltpu.VMEM((flat, rows), f32),
            pltpu.VMEM((strips, flat, LANES), f32),
            pltpu.VMEM((flat, rows), f32),
            pltpu.VMEM((3, 1, count), i32),
            pltpu.VMEM((3, 1, count), f32),
            pltpu.VMEM((3, 1, count), f32),
            pltpu.VMEM((strips, 64, LANES), f32),
            eight,
            eight,
            pltpu.VMEM((count // HALF, groups, 2, HALF), f32),
            pltpu.VMEM((2, count // HALF, groups, 2, HALF), f32),
            pltpu.VMEM((PASSES + 1, 19, tall, rows), f32),
            pltpu.VMEM((n_ens, 4, 8, rows), f32),
            eight,
            pltpu.VMEM((n_ens, 8, 8, rows), f32),
            eight, eight, eight,
            pltpu.VMEM((3, HALF, count), bf16),
            pltpu.VMEM((flat, count), bf16),
            dma((9,)), dma((2, 3)), dma((2, 3)),
            dma((2,)), dma((2,)), dma((2,)), dma((2,)),
            dma((2, count // HALF // 2)), dma((2, count // HALF // 2)),
            dma((n_ens,)), dma((n_ens,)),
            dma((2,)), dma((2,)),
            dma((2, n_ens)), dma((2, n_ens)), dma((2, n_ens)), dma((2, n_ens)),
        ],
        compiler_params=pltpu.CompilerParams(
            collective_id=0, has_side_effects=True, vmem_limit_bytes=60 * 2**20
        ),
        name="exchange",
    )(
        class_kappa, alpha.reshape(flat, rows), perturb.reshape(flat, rows),
        static_ctl.reshape(32, rows), sigma.reshape(32, rows), class_index.reshape(32, rows),
        obs_cell.reshape(1, count), obs_value.reshape(1, count), obs_weight.reshape(1, count),
    )
    ga, gs = pl.pallas_call(
        functools.partial(adjoint, scale),
        out_shape=(
            jax.ShapeDtypeStruct((flat, rows), f32),
            jax.ShapeDtypeStruct((32, rows), f32),
        ),
        in_specs=[vmem] * len(fields),
        out_specs=(hbm,) * 2,
        scratch_shapes=[
            pltpu.VMEM((flat, rows), f32),
            pltpu.VMEM((strips, flat, LANES), f32),
            pltpu.VMEM((strips, 32, LANES), f32),
            pltpu.VMEM((32, rows), f32),
            pltpu.VMEM((19, tall, rows), f32),
            dma((2,)), dma(()),
        ],
        compiler_params=pltpu.CompilerParams(vmem_limit_bytes=24 * 2**20),
        name="adjoint",
    )(*passed)
    return ga.reshape(alpha.shape), gs.reshape(static_ctl.shape)


def solution(mesh):
    return jax.shard_map(
        per_device,
        mesh=mesh,
        in_specs=(
            P("ens", None, "dom", None),
            P("ens", None, "dom", None),
            P(None, "dom", None),
            P(None, "dom", None),
            P(None, "dom", None),
            P(),
            P("dom"),
            P("dom"),
            P("dom"),
        ),
        out_specs=(P("ens", None, "dom", None), P(None, "dom", None)),
        check_vma=False,
    )
```

```python
import functools
import math

import jax
import jax.numpy as jnp
from jax import lax
from jax.experimental import pallas as pl
from jax.experimental.pallas import tpu as pltpu
from jax.sharding import PartitionSpec as P

PASSES = 4
MESH = pl.DeviceIdType.MESH
LANES = 128
HALF = 256
PIECES = 3
CHUNKS = 4
f32 = jnp.float32
bf16 = jnp.bfloat16


def sub(shape):
    return lax.broadcasted_iota(jnp.int32, shape, len(shape) - 2)


def low_rows(shape):
    return sub(shape) < 4


def flip(x):
    return pltpu.roll(x, 4, 0)


def pair(a, b):
    return jnp.where(low_rows(a.shape), a, b)


def spread(x):
    other, low = flip(x), low_rows(x.shape)
    return jnp.where(low, x, other), jnp.where(low, other, x)


def march(old, new, fx, fy, wrap, first, quads):
    groups = old.shape[1] // 8
    strips = fx.shape[-1] // LANES

    def get(ref, c, g=0):
        return [ref[c, 8 * g : 8 * g + 8, block(v)] for v in range(strips)]

    def body(i, left):
        c0 = first + 1 + 4 * i
        us = [[get(old, c0 + k, g) for g in range(groups)] for k in range(5)]
        after = [[pltpu.roll(us[k][g][0], LANES - 1, 1) for g in range(groups)] for k in range(4)]
        before = [[pltpu.roll(us[k][g][-1], 1, 1) for g in range(groups)] for k in range(4)]
        out = []
        for k in range(4):
            face, side, first_side = get(fx, c0 + k), get(fy, c0 + k), wrap[c0 + k]
            fluxes = []
            for g in range(groups):
                u, there = us[k][g], us[k + 1][g]
                right = [f * (b - a) for f, a, b in zip(face, u, there, strict=True)]
                up = [f * (b - a) for f, a, b in zip(side, u, u[1:] + [after[k][g]], strict=True)]
                down = [first_side * (u[0] - before[k][g])] + up[:-1]
                out.append([
                    a + (x - y) + (p - q)
                    for a, x, y, p, q in zip(u, right, left[g], up, down, strict=True)
                ])
                fluxes.append(right)
            left = fluxes
        for k in range(4):
            for g in range(groups):
                for v in range(strips):
                    new[c0 + k, 8 * g : 8 * g + 8, block(v)] = out[k * groups + g][v]
        return left

    start = [
        [f * (b - a) for f, a, b in zip(get(fx, first), get(old, first, g), get(old, first + 1, g), strict=True)]
        for g in range(groups)
    ]
    lax.fori_loop(0, quads, body, start)


def spot(cell):
    return (cell & -512) | ((cell & 3) << 7) | ((cell & 511) >> 2)


def order_rows(x, order):
    pieces = [piece.astype(bf16) for piece in split3(x)]
    every = jnp.dot(jnp.concatenate(pieces[::-1], axis=0), order[...], preferred_element_type=f32)
    n = x.shape[0]
    return (every[:n] + every[n : 2 * n]) + every[2 * n :]


def natural_rows(x, order):
    high = x.astype(bf16)
    low = (x - high.astype(f32)).astype(bf16)
    both = lax.dot_general(
        jnp.concatenate([low, high], axis=0), order[...], (((1,), (1,)), ((), ())), preferred_element_type=f32
    )
    return both[: x.shape[0]] + both[x.shape[0] :]


def split3(x):
    out = []
    for _ in range(PIECES):
        out.append(x.astype(bf16).astype(f32))
        x = x - out[-1]
    return out


def block(v):
    return slice(v * LANES, (v + 1) * LANES)


def take(ref, at, count=8):
    return jnp.concatenate(
        [ref[v, pl.ds(at, count, stride=8), :] for v in range(ref.shape[0])], axis=1
    )


def put(ref, at, value):
    for v in range(ref.shape[0]):
        ref[v, pl.ds(at, value.shape[0], stride=8), :] = value[:, block(v)]


def lanes_of(t):
    return pl.ds(pl.multiple_of(t * LANES, LANES), LANES)


def hot_rows(cell, hot, t):
    low = (cell & (HALF - 1)).astype(f32)
    spot = lax.broadcasted_iota(jnp.int32, (HALF, LANES), 0).astype(f32)
    hot[:, lanes_of(t)] = jnp.where(spot == low, 1.0, 0.0).astype(bf16)


def exchange(
    n_dom, n_ens, scale,
    kappa_in, alpha_in, perturb_in, static_in, sigma_in, index_in, cell_in, value_in, weight_in,
    adj, member, fx, fy, wrap, order, alpha, static, sigma,
    kappa, index, perturb, ordered, wide, natural, cells, values, weights, twice, edge, known, p_send, p_recv,
    field, shared, plain, tails, w_all, v_all, n_all, hot, x_all,
    in_sem, o_ss, o_rs, c_ss, c_rs, k_ss, k_rs, p_ss, p_rs, s_ss, s_rs, i_ss, i_rs, t_ss, t_rs, m_ss, m_rs,
):
    me, ens = lax.axis_index("dom"), lax.axis_index("ens")
    right, left = lax.rem(me + 1, n_dom), lax.rem(me + n_dom - 1, n_dom)
    rows = fx.shape[-1]
    strips = rows // LANES
    groups = member.shape[1] // 8
    deep = cells.shape[-1] // HALF
    sides = ((0, left), (1, right))

    barrier = pltpu.get_barrier_semaphore()
    for side in (right, left):
        for r in range(n_ens):
            pl.semaphore_signal(
                barrier, inc=1, device_id=(side, lax.rem(ens + r, n_ens)), device_id_type=MESH
            )
    for r in range(1, n_ens):
        pl.semaphore_signal(
            barrier, inc=1, device_id=(me, lax.rem(ens + r, n_ens)), device_id_type=MESH
        )

    loads = [
        pltpu.make_async_copy(src, dst, in_sem.at[i])
        for i, (src, dst) in enumerate((
            (index_in, index), (kappa_in, kappa), (cell_in, cells.at[2]), (perturb_in, perturb),
            (static_in, static), (sigma_in, sigma), (weight_in, weights.at[2]), (value_in, values.at[2]),
            (alpha_in, alpha),
        ))
    ]
    for copy in loads:
        copy.start()

    def remote(src, dst, ss, rs, side, r=0):
        return pltpu.make_async_remote_copy(
            src_ref=src, dst_ref=dst, send_sem=ss, recv_sem=rs,
            device_id=(side, lax.rem(ens + r, n_ens)), device_id_type=MESH,
        )

    def started(copies):
        for copy in copies:
            copy.start()
        return copies

    def swap(ref, ss, rs):
        return [
            remote(ref.at[pl.ds(2 + 2 * s, 2)], ref.at[pl.ds(6 - 6 * s, 2)], ss.at[s], rs.at[1 - s], side)
            for s, side in sides
        ]

    def pairs_of(value, out):
        for v in range(strips):
            for level in range(4):
                tile = value(level, v)
                twice[v, 8 * level : 8 * level + 8, :] = tile
                twice[v, 32 + 8 * level : 40 + 8 * level, :] = tile
        for v in range(strips):
            for j in range(4):
                a, b = [twice[v, pl.ds(2 * j + i, 8, stride=8), :] for i in range(2)]
                out[2 + j, :, block(v)] = pair(a, b)

    zero = jnp.zeros((8, rows), f32)

    def sort_rows(v, carry):
        row = lax.broadcasted_iota(jnp.int32, (LANES, rows), 0) + v * LANES
        to = ((row & 3) << 7) | (row >> 2)
        here = lax.broadcasted_iota(jnp.int32, (LANES, rows), 1)
        order[pl.ds(pl.multiple_of(v * LANES, LANES), LANES), :] = jnp.where(to == here, 1.0, 0.0).astype(bf16)
        return carry

    lax.fori_loop(0, strips, sort_rows, 0)

    def clear(g, carry):
        at = pl.ds(pl.multiple_of(8 * g, 8), 8)
        for p, outer in ((0, (3, 4, 13, 14, 15, 16)), (1, (2, 3)), (2, (1, 2, 15, 16, 17, 18)), (3, (0, 1))):
            for c in outer:
                field[p, c, at] = zero
        return carry

    lax.fori_loop(0, groups, clear, 0)

    loads[0].wait()
    loads[1].wait()
    number = jnp.dot(index[...].astype(f32).astype(bf16), order[...], preferred_element_type=f32)

    def coefficient(level, v):
        mine = number[8 * level : 8 * level + 8, block(v)]
        out = jnp.zeros((8, LANES), f32)
        for k in range(kappa.shape[0]):
            out = jnp.where(mine == k, kappa[k], out)
        return out

    pairs_of(coefficient, edge)

    def pass_on(src, dst, i):
        return [remote(src, dst.at[1 - s], o_ss.at[s, i], o_rs.at[1 - s, i], side) for s, side in sides]

    edge_copies = swap(edge, c_ss, c_rs)
    first_copies = edge_copies + pass_on(cell_in, cells, 0)

    def greet(now):
        @pl.when(now)
        def _():
            pl.semaphore_wait(barrier, 3 * n_ens - 1)
            for copy in first_copies:
                copy.start()

    greet(me != 0)
    loads[3].wait()
    ordered[...] = jnp.dot(perturb[...], order[...], preferred_element_type=f32)
    perturb[...] = ordered[...].astype(bf16)
    loads[2].wait()

    def collect(n, carry):
        for i in range(4):
            hot_rows(spot(cells[2, :, lanes_of(4 * n + i)]), hot.at[2], 4 * n + i)
        span = pl.ds(pl.multiple_of(n * 2 * HALF, 2 * HALF), 2 * HALF)
        found = [
            lax.dot_general(
                perturb[:, h * HALF : (h + 1) * HALF], hot[2, :, span],
                (((1,), (0,)), ((), ())), preferred_element_type=f32,
            )
            for h in range(2)
        ]
        column = sub((8, LANES)) * 2
        for i in range(4):
            key = lax.shift_right_logical(spot(cells[2, :, lanes_of(4 * n + i)]), 8)
            masks = [[column + (16 * level + h) == key for h in range(2)] for level in range(4)]
            for m in range(2 * groups):
                kept = jnp.zeros((8, LANES), f32)
                for level in range(4):
                    for h in range(2):
                        at = (m * 4 + level) * 8
                        piece = found[h][at : at + 8, block(i)]
                        kept = jnp.where(masks[level][h], piece, kept)
                p_send[2 * n + i // 2, m // 2, m % 2 : m % 2 + 1, block(i % 2)] = jnp.sum(
                    kept, axis=0, keepdims=True
                )
        return carry

    def p_copy(s, side, n):
        part = pl.ds(2 * n, 2)
        return remote(p_send.at[part], p_recv.at[1 - s, part], p_ss.at[s, n], p_rs.at[1 - s, n], side)

    def collect_and_send(n, carry):
        collect(n, carry)

        @pl.when(me != 0)
        def _():
            started([p_copy(s, side, n) for s, side in sides])

        return carry

    lax.fori_loop(0, deep // 2, collect_and_send, 0)

    greet(me == 0)
    pl.when(me == 0)(lambda: started([p_copy(0, left, n) for n in range(deep // 2)]) and None)

    loads[4].wait()
    loads[5].wait()
    product = order_rows(static[...] * sigma[...], order)
    pairs_of(lambda level, v: product[8 * level : 8 * level + 8, block(v)], known)
    pl.when(me == 0)(lambda: started([p_copy(1, right, n) for n in range(deep // 2)]) and None)

    for v in range(strips):
        wide[v] = ordered[:, block(v)]

    def arrange(ref, at):
        def column(c, carry):
            for g in range(groups):
                ref[at + c, 8 * g : 8 * g + 8] = take(wide, g * 64 + c)
            return carry

        lax.fori_loop(0, 8, column, 0)

    arrange(member, 4)
    loads[8].wait()
    natural[...] = order_rows(alpha[...], order)
    for v in range(strips):
        wide[v] = natural[:, block(v)]
    arrange(field.at[0], 5)

    column_pairs = (sub((8, LANES)) % 4) * 16 + (sub((8, LANES)) // 4) * 2

    def weigh(q, carry):
        slot = jnp.where(q == 0, 0, jnp.where(q == 3, 1, 2))
        first = 2 * (1 - q % 2)

        def fill(t, carry):
            at = lanes_of(t)
            key = lax.shift_right_logical(spot(cells[slot, :, at]), 8)
            weight = weights[slot, :, at]
            pieces = split3(weight) + split3(weight * values[slot, :, at]) + [jnp.ones_like(weight)]
            masks = [column_pairs + (4 * (first + n) + h) == key for h in range(2) for n in range(2)]
            out = [jnp.where(mask, piece, 0.0) for piece in pieces for mask in masks]
            x_all[0 : 8 * len(out), at] = jnp.concatenate(out, axis=0).astype(bf16)
            return carry

        lax.fori_loop(0, 2 * deep, fill, 0)
        sums = lax.dot_general(
            x_all[0 : 7 * 32, :], hot[slot], (((1,), (1,)), ((), ())), preferred_element_type=f32
        )
        part = [sums[i * 32 : (i + 1) * 32] for i in range(7)]
        for ref, value in (
            (w_all, (part[2] + part[1]) + part[0]), (v_all, (part[5] + part[4]) + part[3]), (n_all, part[6])
        ):
            for h in range(2):
                for n in range(2):
                    row = (h * 2 + n) * 8
                    ref[2 * q + n, :, h * HALF : (h + 1) * HALF] = value[row : row + 8]
        return carry


    lane = lax.broadcasted_iota(jnp.int32, (8, LANES), 1)

    def faces(j, previous):
        for i, here in enumerate(spread(edge[j])):
            c = 2 * j + i
            blocks = [here[:, block(v)] for v in range(strips)]
            after = blocks[1:] + [pltpu.roll(blocks[0], LANES - 1, 1)]
            up = [0.5 * (a + b) for a, b in zip(blocks, after, strict=True)]
            up[-1] = jnp.where(lane < LANES - 1, up[-1], 0.0)
            for v in range(strips):
                fy[c + 1, :, block(v)] = up[v]
            wrap[c + 1] = pltpu.roll(up[-1], 1, 1)
            fx[c] = 0.5 * (previous + here)
            previous = here
        return previous


    def forward(p, carry):
        march(field.at[p], field.at[p + 1], fx, fy, wrap, 3 - p, 2)
        return carry

    def forward_right(p, carry):
        march(field.at[p], field.at[p + 1], fx, fy, wrap, 11 - p, 1 + p // 2)
        return carry

    def both(x):
        return x + flip(x)

    def gather(j):
        sums = []
        for i in range(2):
            c = 2 * j + i
            acc = member[c, 0:8] * field[PASSES, c + 1, 0:8]
            for g in range(1, groups):
                acc = acc + member[c, 8 * g : 8 * g + 8] * field[PASSES, c + 1, 8 * g : 8 * g + 8]
            sums.append(both(acc))
        return pair(*sums)

    def inner(j, carry):
        shared[0, j] = gather(j + 2)
        return carry

    own_copies = [
        remote(shared.at[0], shared.at[r], s_ss.at[r], s_rs.at[r], me, r) for r in range(1, n_ens)
    ]

    def spread_left():
        edge_copies[1].wait()
        lax.fori_loop(0, 6, faces, zero)
        fx[0] = zero
        lax.fori_loop(0, PASSES, forward, 0)

    def spread_right():
        edge_copies[0].wait()
        lax.fori_loop(6, 8, faces, spread(edge[5])[1])
        fx[16], fx[17], fy[17], wrap[17] = zero, zero, zero, zero[:, block(0)]
        lax.fori_loop(0, PASSES, forward_right, 0)
        lax.fori_loop(0, 4, inner, 0)
        started(own_copies)

    level_of = (sub((8, LANES)) % 4) * 16
    upper = sub((8, LANES)) < 4

    def tail_copies(s, side):
        return [
            pltpu.make_async_remote_copy(
                src_ref=tails.at[0, pl.ds(6 * s, 2)], dst_ref=tails.at[r, pl.ds(4 - 2 * s, 2)],
                send_sem=t_ss.at[s, r], recv_sem=t_rs.at[1 - s, r],
                device_id=(side, lax.rem(ens + r, n_ens)), device_id_type=MESH,
            )
            for r in range(n_ens)
        ] + [
            pltpu.make_async_remote_copy(
                src_ref=tails.at[0, pl.ds(6 * s, 2)], dst_ref=tails.at[r, pl.ds(6 * s, 2)],
                send_sem=m_ss.at[s, r], recv_sem=m_rs.at[s, r],
                device_id=(me, lax.rem(ens + r, n_ens)), device_id_type=MESH,
            )
            for r in range(1, n_ens)
        ]

    plain_copies = swap(plain, i_ss, i_rs)

    def settle():
        for copy in own_copies:
            copy.wait()
        for j in range(4):
            whole = shared[lax.rem(ens + n_ens, n_ens), j]
            for e in range(1, n_ens):
                whole = whole + shared[lax.rem(ens - e + n_ens, n_ens), j]
            plain[2 + j] = whole
        started(plain_copies)

    final = me == n_dom - 1

    def beside(s, i):
        away = jnp.where(s == 0, right, left)
        remote(cell_in, cells.at[s], o_ss.at[1 - s, 0], o_rs.at[s, 0], away).wait()

        def place(t, carry):
            cell = spot(cells[s, :, lanes_of(t)])
            hot_rows(cell, hot.at[s], t)
            key = lax.shift_right_logical(cell, 8)
            at = lanes_of(t % 2)
            value = [
                jnp.where(upper, p_recv[s, t // 2, g, 0:1, at], p_recv[s, t // 2, g, 1:2, at])
                for g in range(groups)
            ]
            out = []
            for h in range(2):
                for c in range(4):
                    mask = level_of + (2 * (c + 4 - 4 * s) + h) == key
                    out += [jnp.where(mask, v, 0.0) for v in value]
            x_all[:, lanes_of(t)] = jnp.concatenate(out, axis=0).astype(bf16)
            return carry

        def part(n, carry):
            p_copy(1 - s, away, n).wait()
            return lax.fori_loop(4 * n, 4 * n + 4, place, carry)

        lax.fori_loop(0, deep // 2, part, 0)
        pl.when(i == jnp.where(final, 2, 1))(settle)
        found = lax.dot_general(
            x_all[...], hot[s], (((1,), (1,)), ((), ())), preferred_element_type=f32
        )
        for h in range(2):
            for c in range(4):
                for g in range(groups):
                    at = ((h * 4 + c) * groups + g) * 8
                    member[12 * s + c, 8 * g : 8 * g + 8, h * HALF : (h + 1) * HALF] = found[at : at + 8]


    def weights_of(own):
        @pl.when(jnp.logical_not(own))
        def _():
            for copy in weight_copies:
                copy.wait()

        lax.fori_loop(0, 2, lambda n, carry: weigh(jnp.where(own, 1 + n, 3 * n), carry), 0)

    def phase(step, carry):
        i = step - jnp.where(me == 0, 1, 0)
        working = jnp.logical_and(i >= 0, i < 3)
        pl.when(jnp.logical_not(working))(lambda: weights_of(step == jnp.where(me == 0, 0, 3)))
        pl.when(working)(lambda: sided(i))
        return carry

    def sided(i):
        stencil = i == jnp.where(final, 1, 0)
        s = jnp.where(final, i // 2, jnp.where(me < 2, 2 - i, i - 1))
        pl.when(stencil)(spread_right)
        pl.when(jnp.logical_not(stencil))(lambda: beside(s, i))

        def tail(n, carry):
            out = jnp.where(final, 1 - n, s)
            for j in range(2):
                tails[0, 6 * out + j] = gather(6 * out + j)
            started(tail_copies(out, jnp.where(out == 0, left, right)))
            return carry

        lax.fori_loop(0, jnp.where(final, i // 2 * 2, jnp.minimum(i, 1)), tail, 0)

    loads[6].wait()
    loads[7].wait()
    spread_left()
    weight_copies = started(pass_on(weight_in, weights, 1) + pass_on(value_in, values, 2))
    known_copies = started(swap(known, k_ss, k_rs))
    lax.fori_loop(0, 5, phase, 0)

    for copy in known_copies + plain_copies + tail_copies(0, left) + tail_copies(1, right):
        copy.wait()

    def finish(j, carry):
        once = 1.0 / jnp.maximum(n_all[j], 1.0)
        whole = tails[lax.rem(ens + n_ens, n_ens), j]
        for e in range(1, n_ens):
            whole = whole + tails[lax.rem(ens - e + n_ens, n_ens), j]
        state = known[j] + scale * (plain[j] + whole * once)
        tile = w_all[j] * state - v_all[j]
        own = jnp.logical_and(j >= 2, j < 6)
        tile = jnp.where(own, tile, tile * once)
        adj[2 * j], adj[2 * j + 1] = spread(tile)
        return carry

    lax.fori_loop(0, 8, finish, 0, unroll=4)


def adjoint(
    scale, adj, member, fx, fy, wrap, order, alpha, static, sigma,
    ga, gs, out, wide, small, result, field, ga_sem, gs_sem,
):
    groups = member.shape[1] // 8
    strips = wide.shape[0]

    def begin(c, carry):
        one = adj[c]
        for g in range(groups):
            field[c + 1, 8 * g : 8 * g + 8] = member[c, 8 * g : 8 * g + 8] * one
        return carry

    lax.fori_loop(0, 16, begin, 0)

    def back(p, carry):
        march(field, field, fx, fy, wrap, p + 1, (17 - 2 * p) // 4)
        return carry

    lax.fori_loop(0, PASSES, back, 0)

    def end(c, carry):
        for g in range(groups):
            put(wide, g * 64 + c, field[5 + c, 8 * g : 8 * g + 8])
        put(small, c, adj[4 + c][0:4])
        return carry

    lax.fori_loop(0, 8, end, 0)

    def joined(ref, at):
        return jnp.concatenate([ref[v, at] for v in range(strips)], axis=1)

    whole = wide.shape[1]
    first = 32 * groups
    at = pl.ds(0, first)
    out[at] = alpha[at] + scale * natural_rows(joined(wide, at), order)
    copies = [pltpu.make_async_copy(out.at[at], ga.at[at], ga_sem.at[0])]
    copies[0].start()
    at = pl.ds(first, whole - first)
    rest = natural_rows(jnp.concatenate([joined(wide, at), joined(small, slice(None))], axis=0), order)
    out[at] = alpha[at] + scale * rest[: whole - first]
    copies.append(pltpu.make_async_copy(out.at[at], ga.at[at], ga_sem.at[1]))
    copies[1].start()
    result[...] = static[...] + sigma[...] * rest[whole - first :]
    copies.append(pltpu.make_async_copy(result, gs, gs_sem))
    copies[2].start()
    for copy in copies:
        copy.wait()


def per_device(
    alpha, perturb, static_ctl, sigma, class_index, class_kappa, obs_cell, obs_value, obs_weight
):
    n_dom, n_ens = lax.axis_size("dom"), lax.axis_size("ens")
    local, levels, columns, rows = alpha.shape
    assert columns == 8 and levels == 4 and rows == 512 and local % 2 == 0
    scale = 1.0 / math.sqrt(local * n_ens - 1)
    count = obs_cell.shape[0]
    groups = local // 2
    flat = local * 32
    tall = groups * 8
    strips = rows // LANES
    hbm = pl.BlockSpec(memory_space=pltpu.HBM)
    vmem = pl.BlockSpec(memory_space=pltpu.VMEM)
    dma = pltpu.SemaphoreType.DMA
    i32 = jnp.int32
    eight = pltpu.VMEM((8, 8, rows), f32)
    fields = (
        pltpu.VMEM((16, 8, rows), f32),
        pltpu.VMEM((16, tall, rows), f32),
        pltpu.VMEM((18, 8, rows), f32),
        pltpu.VMEM((18, 8, rows), f32),
        pltpu.VMEM((18, 8, LANES), f32),
        pltpu.VMEM((rows, rows), bf16),
        pltpu.VMEM((flat, rows), f32),
        pltpu.VMEM((32, rows), f32),
        pltpu.VMEM((32, rows), f32),
    )
    passed = pl.pallas_call(
        functools.partial(exchange, n_dom, n_ens, scale),
        out_shape=fields,
        in_specs=[hbm] * 9,
        out_specs=(vmem,) * len(fields),
        scratch_shapes=[
            pltpu.SMEM(class_kappa.shape, f32),
            pltpu.VMEM((32, rows), i32),
            pltpu.VMEM((flat, rows), bf16),
            pltpu.VMEM((flat, rows), f32),
            pltpu.VMEM((strips, flat, LANES), f32),
            pltpu.VMEM((flat, rows), f32),
            pltpu.VMEM((3, 1, count), i32),
            pltpu.VMEM((3, 1, count), f32),
            pltpu.VMEM((3, 1, count), f32),
            pltpu.VMEM((strips, 64, LANES), f32),
            eight,
            eight,
            pltpu.VMEM((count // HALF, groups, 2, HALF), f32),
            pltpu.VMEM((2, count // HALF, groups, 2, HALF), f32),
            pltpu.VMEM((PASSES + 1, 19, tall, rows), f32),
            pltpu.VMEM((n_ens, 4, 8, rows), f32),
            eight,
            pltpu.VMEM((n_ens, 8, 8, rows), f32),
            eight, eight, eight,
            pltpu.VMEM((3, HALF, count), bf16),
            pltpu.VMEM((flat, count), bf16),
            dma((9,)), dma((2, 3)), dma((2, 3)),
            dma((2,)), dma((2,)), dma((2,)), dma((2,)),
            dma((2, count // HALF // 2)), dma((2, count // HALF // 2)),
            dma((n_ens,)), dma((n_ens,)),
            dma((2,)), dma((2,)),
            dma((2, n_ens)), dma((2, n_ens)), dma((2, n_ens)), dma((2, n_ens)),
        ],
        compiler_params=pltpu.CompilerParams(
            collective_id=0, has_side_effects=True, vmem_limit_bytes=60 * 2**20
        ),
        name="exchange",
    )(
        class_kappa, alpha.reshape(flat, rows), perturb.reshape(flat, rows),
        static_ctl.reshape(32, rows), sigma.reshape(32, rows), class_index.reshape(32, rows),
        obs_cell.reshape(1, count), obs_value.reshape(1, count), obs_weight.reshape(1, count),
    )
    ga, gs = pl.pallas_call(
        functools.partial(adjoint, scale),
        out_shape=(
            jax.ShapeDtypeStruct((flat, rows), f32),
            jax.ShapeDtypeStruct((32, rows), f32),
        ),
        in_specs=[vmem] * len(fields),
        out_specs=(hbm,) * 2,
        scratch_shapes=[
            pltpu.VMEM((flat, rows), f32),
            pltpu.VMEM((strips, flat, LANES), f32),
            pltpu.VMEM((strips, 32, LANES), f32),
            pltpu.VMEM((32, rows), f32),
            pltpu.VMEM((19, tall, rows), f32),
            dma((2,)), dma(()),
        ],
        compiler_params=pltpu.CompilerParams(vmem_limit_bytes=24 * 2**20),
        name="adjoint",
    )(*passed)
    return ga.reshape(alpha.shape), gs.reshape(static_ctl.shape)


def solution(mesh):
    return jax.shard_map(
        per_device,
        mesh=mesh,
        in_specs=(
            P("ens", None, "dom", None),
            P("ens", None, "dom", None),
            P(None, "dom", None),
            P(None, "dom", None),
            P(None, "dom", None),
            P(),
            P("dom"),
            P("dom"),
            P("dom"),
        ),
        out_specs=(P("ens", None, "dom", None), P(None, "dom", None)),
        check_vma=False,
    )
```
